32 devices in a mesh: blk: 8 (over z, x), slab: 4 (over y, core).
Axes of the slice: x: 2, y: 2, z: 4, core: 2. Of those that a mesh axis runs over, the one named last changes fastest.
Arguments:
- xinv: bfloat16 [8, 4096, 4096], P('blk', None, 'slab'), may hold values from -1 to 16
- ymat: bfloat16 [8, 4096, 4096], P('blk', None, 'slab'), may hold values from -1 to 16
- basis: bfloat16 [8, 4096, 1024], P('blk', 'slab'), may hold values from -0.08118988 to 0.08118988
- pair_index: int32 [8, 2, 512], P('blk'), may hold values from 0 to 1023
- orders: int32 [8], replicated, may hold values from 1 to 512, 2048 in all
- dest: int32 [8], replicated, may hold values from 0 to 7, each once
Outputs:
- factor: float32 [8, 512, 512], P('blk', 'slab')
The draws below stay inside these ranges and needn't reach their ends.
Inputs may be any that keep to these rules, and one draw needn't show every extreme that they name: `pair_index`: entries name columns of the block's basis. Sum of all orders is 2048; the largest equals 512. `dest`: every group receives exactly one block.
All inputs are finite; a program needn't handle non-finite values.
Results may differ from the reference program's by a relative error of at most 0.0003.
Values may be sent and summed in bfloat16 or wider, within the bound.
No kernel may reach another device: no remote copies, remote signals or barrier semaphores. Data moves between devices by JAX's collectives and lax.ppermute only.
A program may use at most 64 MiB of HBM per device.

```python
import math
import jax
import jax.numpy as jnp
import numpy as np
from jax import lax

P_SIZE = 4096
R = 1024
MMAX = 512
BLOCKS = 8


shared_rank = 16


def positive_blocks(key):
    key_off, key_diag = jax.random.split(key, 2)
    noise = jax.random.normal(key_off, (BLOCKS, P_SIZE, P_SIZE), jnp.float32) * (0.2 / (2.0 * P_SIZE) ** 0.5)
    sym = noise + jnp.swapaxes(noise, 1, 2)
    diag = jnp.exp(jax.random.uniform(key_diag, (BLOCKS, P_SIZE), jnp.float32, 0.0, 1.386))
    eye = (jnp.arange(P_SIZE)[:, None] == jnp.arange(P_SIZE)[None, :]).astype(jnp.float32)
    whole = sym + eye[None] * diag[:, :, None]
    return whole


def draw_xinv(key, part):
    return positive_blocks(jax.random.fold_in(key, 11)).astype(jnp.bfloat16)


def draw_ymat(key, part):
    return positive_blocks(jax.random.fold_in(key, 23)).astype(jnp.bfloat16)


def draw_basis(key, part):
    key_noise, key_left, key_mix = jax.random.split(jax.random.fold_in(key, 37), 3)
    spread = 1.0 / P_SIZE ** 0.5
    shared_left = jax.random.normal(key_left, (BLOCKS, P_SIZE, shared_rank), jnp.float32) * spread
    shared_mix = jax.random.normal(key_mix, (BLOCKS, shared_rank, R), jnp.float32) * 0.34
    shared_part = jnp.einsum('bpk,bkr->bpr', shared_left, shared_mix, precision=lax.Precision.HIGHEST)
    own_part = jax.random.normal(key_noise, (BLOCKS, P_SIZE, R), jnp.float32) * spread
    whole = own_part + shared_part
    largest = (27.0 / P_SIZE) ** 0.5
    return jnp.clip(whole, -largest, largest).astype(jnp.bfloat16)


def with_ends(entries, stream_key, low, high):
    place = [jax.random.randint(jax.random.fold_in(stream_key, axis), (), 0, length) for axis, length in enumerate(entries.shape)]
    main_axis = entries.shape.index(max(entries.shape))
    next_to = place[:main_axis] + [(place[main_axis] + 1) % entries.shape[main_axis]] + place[main_axis + 1:]
    return entries.at[tuple(place)].set(low).at[tuple(next_to)].set(high)


def profile(count, total, reach, lean):
    weights = [(1 << 20) // math.isqrt(grade ** lean) + 1 for grade in range(2, count + 1)]
    spare, counts = total - reach - (count - 1), [1] * (count - 1)
    while spare > 0:
        free = [i for i in range(count - 1) if counts[i] < reach]
        whole, budget = sum([weights[i] for i in free]), spare
        for i in free:
            more = min(reach - counts[i], max(1, budget * weights[i] // whole), spare)
            counts[i] = counts[i] + more
            spare = spare - more
    return np.array([reach] + counts)


def ragged_sizes(rng, amount, total, reach, slope):
    if amount == 2:
        one = jax.random.randint(rng, (), max(1, total - reach), min(reach, total - 1) + 1)
        return jnp.stack([one, total - one])
    lengths = jnp.asarray(profile(amount, total, reach, slope), jnp.int32)
    twos = (amount - 1) // 2
    source_of, taker = lengths[1:1 + 2 * twos:2], lengths[2:2 + 2 * twos:2]
    slack = jnp.minimum(source_of - 1, reach - taker)
    shifted = jax.random.randint(jax.random.fold_in(rng, 1), (twos,), 0, 1 << 20) % (slack + 1)
    lengths = lengths.at[1:1 + 2 * twos:2].set(source_of - shifted).at[2:2 + 2 * twos:2].set(taker + shifted)
    return lengths[jax.random.permutation(jax.random.fold_in(rng, 2), amount)]


def setup_inputs(seed: int = 0) -> dict:
    streams_of = jax.random.split(jax.random.key(seed), 7)
    xinv = draw_xinv(jax.random.fold_in(streams_of[6], 71), 0)
    ymat = draw_ymat(jax.random.fold_in(streams_of[6], 71), 0)
    basis = draw_basis(jax.random.fold_in(streams_of[6], 71), 0)
    pair_index = with_ends(jax.random.randint(streams_of[3], (BLOCKS, 2, MMAX), 0, R), jax.random.fold_in(streams_of[3], 1), 0, R - 1).astype(jnp.int32)
    orders = ragged_sizes(streams_of[4], BLOCKS, BLOCKS * MMAX // 2, MMAX, 2).astype(jnp.int32)
    dest = jax.random.permutation(streams_of[5], BLOCKS).astype(jnp.int32)
    return {"xinv": xinv, "ymat": ymat, "basis": basis, "pair_index": pair_index, "orders": orders, "dest": dest}


def one_block(operands):
    xblock, yblock, vblock, index, order = operands
    vfloat = vblock.astype(jnp.float32)
    high = lax.Precision.HIGHEST
    cx = jnp.dot(vfloat.T, xblock.astype(jnp.float32), precision=high).astype(jnp.bfloat16)
    cy = jnp.dot(vfloat.T, yblock.astype(jnp.float32), precision=high).astype(jnp.bfloat16)
    cx = lax.optimization_barrier(cx)
    cy = lax.optimization_barrier(cy)
    apair = jnp.dot(cx.astype(jnp.float32), vfloat, precision=high)
    bpair = jnp.dot(cy.astype(jnp.float32), vfloat, precision=high)
    first = index[0]
    second = index[1]
    a_rows = apair[first]
    b_rows = bpair[second]
    schur = a_rows[:, first] * b_rows[:, second]
    live = jnp.arange(MMAX, dtype=jnp.int32) < order
    mask = live[:, None] & live[None, :]
    whole = jnp.where(mask, schur, 0.0) + jnp.eye(MMAX, dtype=jnp.float32)
    return jnp.linalg.cholesky(whole)

def reference(xinv, ymat, basis, pair_index, orders, dest):
    factors = lax.map(one_block, (xinv, ymat, basis, pair_index, orders))
    placed = jnp.zeros_like(factors).at[dest].set(factors)
    return placed
```

```python
import functools

import jax
import jax.numpy as jnp
from jax import lax
from jax.experimental import pallas as pl
from jax.experimental.pallas import tpu as pltpu
from jax.sharding import PartitionSpec as P

F32 = jnp.float32
BF16 = jnp.bfloat16
LANES = 128
MICRO = 8
VMEM = pl.BlockSpec(memory_space=pltpu.VMEM)
SMEM = pl.BlockSpec(memory_space=pltpu.SMEM)
TN = (((0,), (0,)), ((), ()))


def dot_f32(a, b, dims):
    dot = functools.partial(lax.dot_general, dimension_numbers=dims, preferred_element_type=F32)
    a_hi, b_hi = a.astype(BF16), b.astype(BF16)
    a_lo = (a - a_hi.astype(F32)).astype(BF16)
    b_lo = (b - b_hi.astype(F32)).astype(BF16)
    return dot(a_hi, b_hi) + (dot(a_hi, b_lo) + dot(a_lo, b_hi))


def lane_splat(x, lane):
    return jnp.broadcast_to(x[:, lane : lane + 1], (MICRO, LANES))


def row_splat(x, row):
    return jnp.broadcast_to(x[row : row + 1, :], (MICRO, x.shape[1]))


def by_tile(f, *wide):
    tiles = [f(*[x[:, t : t + LANES] for x in wide]) for t in range(0, wide[0].shape[1], LANES)]
    return tiles[0] if len(tiles) == 1 else jnp.concatenate(tiles, axis=1)


def factor_rows(a_ref, start, width):
    for m in range(0, LANES, MICRO):
        rows = a_ref[start + m : start + m + MICRO, start : start + width]
        cols = [lane_splat(rows[:, :LANES], m + k) for k in range(MICRO)]
        low = {(i, k): row_splat(cols[k], i) for k in range(MICRO) for i in range(k, MICRO)}
        inv = []
        for k in range(MICRO):
            inv.append(lax.rsqrt(low[k, k]))
            for i in range(k + 1, MICRO):
                low[i, k] = low[i, k] * inv[k]
            for j in range(k + 1, MICRO):
                for i in range(j, MICRO):
                    low[i, j] = low[i, j] - low[i, k] * low[j, k]
        wide = [row_splat(rows, i) for i in range(MICRO)]
        for k in range(MICRO):
            wide[k] = by_tile(lambda x: x * inv[k], wide[k])
            for i in range(k + 1, MICRO):
                wide[i] = by_tile(lambda x, u: x - low[i, k] * u, wide[i], wide[k])
        sub = lax.broadcasted_iota(jnp.int32, (MICRO, width), 0)
        lane = lax.broadcasted_iota(jnp.int32, (MICRO, width), 1)
        packed = wide[0]
        for k in range(1, MICRO):
            packed = jnp.where(sub == k, wide[k], packed)
        a_ref[start + m : start + m + MICRO, start : start + width] = jnp.where(lane >= sub + m, packed, 0.0)
        for later in range(m + MICRO, LANES, MICRO):
            here = pl.ds(start + later, MICRO)
            rest = a_ref[here, start : start + width]
            part = [lane_splat(rest[:, :LANES], m + k) for k in range(MICRO)]
            for k in range(MICRO):
                for j in range(k):
                    part[k] = part[k] - low[k, j] * part[j]
                part[k] = part[k] * inv[k]
            for k in range(MICRO):
                rest = by_tile(lambda x, u: x - part[k] * u, rest, wide[k])
            a_ref[here, start : start + width] = rest


def factor_all(a_ref):
    size = a_ref.shape[0]
    for start in range(0, size, LANES):
        factor_rows(a_ref, start, size - start)
        for row in range(start + LANES, size, LANES):
            left = a_ref[start : start + LANES, row : row + LANES]
            right = a_ref[start : start + LANES, row:]
            a_ref[row : row + LANES, row:] = a_ref[row : row + LANES, row:] - dot_f32(left, right, TN)


def own_rows(a_ref, out_ref, row_start):
    share, size = out_ref.shape
    base = pl.multiple_of(row_start // LANES * LANES, LANES)
    inner = row_start - base
    for q in range(0, size, LANES):
        block = a_ref[q : q + LANES, pl.ds(base, LANES)]
        block = jnp.where(q <= base, block, 0.0).T
        if share % LANES:
            keep = (
                lax.broadcasted_iota(jnp.int32, (share, LANES), 0) + inner
                == lax.broadcasted_iota(jnp.int32, (share, LANES), 1)
            ).astype(F32)
            block = lax.dot_general(
                keep, block, (((1,), (0,)), ((), ())),
                precision=lax.Precision.HIGHEST, preferred_element_type=F32,
            )
        out_ref[:, q : q + LANES] = block


def assemble(block, row, col, order):
    rows = lax.broadcasted_iota(jnp.int32, block.shape, 0) + row
    cols = lax.broadcasted_iota(jnp.int32, block.shape, 1) + col
    return jnp.where((rows < order) & (cols < order), block, 0.0) + (rows == cols).astype(F32)


def upper_blocks(size):
    count = size // LANES
    blocks = [(i, k) for k in range(count) for i in range(k + 1)]
    return blocks[: len(blocks) // 2], blocks[len(blocks) // 2 :]


def factor_kernel(halves, pos_ref, mine_ref, theirs_ref, out_ref, a_ref):
    core, row_start, order = pos_ref[1], pos_ref[2], pos_ref[3]
    for turn in range(2):
        @pl.when(core == turn)
        def _():
            for ref, half in ((mine_ref, halves[turn]), (theirs_ref, halves[1 - turn])):
                for t, (i, k) in enumerate(half):
                    i, k = i * LANES, k * LANES
                    a_ref[i : i + LANES, k : k + LANES] = assemble(ref[t], i, k, order)
    factor_all(a_ref)
    own_rows(a_ref, out_ref, row_start)


def factor_whole_kernel(pos_ref, s_ref, out_ref, a_ref):
    a_ref[...] = s_ref[...]
    factor_all(a_ref)
    own_rows(a_ref, out_ref, pos_ref[2])


def product_kernel(table_ref, pos_ref, x_ref, y_ref, keep_ref, send_ref, out_ref):
    step = pl.program_id(0)
    main, side = pos_ref[0] == 0, table_ref[2, step]
    use_x = jnp.where(side == 0, main, jnp.logical_not(main))

    def put(z_ref, b_ref):
        out_ref[...] = jnp.dot(z_ref[...], b_ref[...], preferred_element_type=F32).astype(BF16)

    pl.when(use_x & (side == 0))(lambda: put(x_ref, keep_ref))
    pl.when(use_x & (side == 1))(lambda: put(x_ref, send_ref))
    pl.when(jnp.logical_not(use_x) & (side == 0))(lambda: put(y_ref, keep_ref))
    pl.when(jnp.logical_not(use_x) & (side == 1))(lambda: put(y_ref, send_ref))


def products(table, pos, x, y, keep, send, tile):
    steps = table.shape[1]
    depth, cols = x.shape[1], keep.shape[1]
    whole = lambda i, table, pos: (0, 0)
    return pl.pallas_call(
        product_kernel,
        out_shape=jax.ShapeDtypeStruct((steps * tile, cols), BF16),
        grid_spec=pltpu.PrefetchScalarGridSpec(
            num_scalar_prefetch=2,
            grid=(steps,),
            in_specs=[
                pl.BlockSpec((tile, depth), lambda i, table, pos: (table[0, i], 0)),
                pl.BlockSpec((tile, depth), lambda i, table, pos: (table[1, i], 0)),
                pl.BlockSpec(keep.shape, whole),
                pl.BlockSpec(send.shape, whole),
            ],
            out_specs=pl.BlockSpec((tile, cols), lambda i, table, pos: (i, 0)),
        ),
        cost_estimate=pl.CostEstimate(
            flops=2 * steps * tile * depth * cols, bytes_accessed=2 * steps * tile * (depth + cols), transcendentals=0
        ),
        name="products",
    )(table, pos, x, y, keep, send)


def scatter_upper(total, halves, core, sym_ref, mine_ref, give_ref):
    sym_ref[...] = total
    count = total.shape[0] // LANES
    for i in range(count):
        for k in range(i, count):
            at = (slice(i * LANES, i * LANES + LANES), slice(k * LANES, k * LANES + LANES))
            mirror = sym_ref[at[1], at[0]].T
            sym_ref[at] = sym_ref[at] + mirror
    for turn in range(2):
        @pl.when(core == turn)
        def _():
            for ref, half in ((mine_ref, halves[turn]), (give_ref, halves[1 - turn])):
                for t, (i, k) in enumerate(half):
                    i, k = i * LANES, k * LANES
                    ref[t] = sym_ref[i : i + LANES, k : k + LANES]


def pair_kernel(halves, scale, pos_ref, *refs):
    count = (len(refs) - 1) // 5
    sym_ref = refs[-1]
    for t in range(count):
        sel_ref, own_ref, other_ref = refs[3 * t : 3 * t + 3]
        mine_ref, give_ref = refs[3 * count + 2 * t : 3 * count + 2 * t + 2]
        both = (own_ref[...].astype(F32) + other_ref[...].astype(F32)).astype(BF16)
        total = lax.dot_general(sel_ref[...], both, TN, preferred_element_type=F32)
        scatter_upper(total * scale, halves, pos_ref[1], sym_ref, mine_ref, give_ref)


def pairings(halves, scale, pos, name, *triples):
    size = triples[0][0].shape[1]
    depth = triples[0][0].shape[0]
    out = []
    for _ in triples:
        out += [jax.ShapeDtypeStruct((len(half), LANES, LANES), F32) for half in (halves[0], halves[1])]
    flat = [x for triple in triples for x in triple]
    return pl.pallas_call(
        functools.partial(pair_kernel, halves, scale),
        out_shape=tuple(out),
        in_specs=[SMEM] + [VMEM] * len(flat),
        out_specs=tuple([VMEM] * len(out)),
        scratch_shapes=[pltpu.VMEM((size, size), F32)],
        cost_estimate=pl.CostEstimate(
            flops=2 * len(triples) * size * size * depth, bytes_accessed=6 * len(triples) * size * depth, transcendentals=0
        ),
        name=name,
    )(pos, *flat)


def select_columns(v, index):
    hot = (lax.broadcasted_iota(jnp.int32, (v.shape[1], index.shape[0]), 0) == index[None, :]).astype(BF16)
    return jnp.dot(v, hot, preferred_element_type=F32).astype(BF16)


def place(own, dest, groups):
    source = jnp.argmax(dest[None, :] == jnp.arange(groups, dtype=dest.dtype)[:, None], axis=1)
    pieces = own.reshape(groups, own.shape[0] // groups, own.shape[1])
    pieces = lax.all_to_all(pieces, "blk", 0, 0)
    pieces = jnp.take(pieces, source, axis=0)
    pieces = lax.all_to_all(pieces, "blk", 0, 0)
    return pieces.reshape(own.shape)


def two_chips(x, y, v, first, second, order, dest):
    slabs, groups = lax.axis_size("slab"), lax.axis_size("blk")
    depth, size = v.shape[0], first.shape[0]
    slab = lax.axis_index("slab")
    chip, core = slab // 2, slab % 2
    halves = upper_blocks(size)
    row_start = slab * (size // slabs)
    pos = jnp.stack([chip, core, row_start, order]).astype(jnp.int32)
    to_core = [(s, s ^ 1) for s in range(slabs)]
    to_chip = [(s, s ^ 2) for s in range(slabs)]

    send = select_columns(v, jnp.where(chip == 0, second, first))
    far = lax.ppermute(send, "slab", to_chip)
    keep = select_columns(v, jnp.where(chip == 0, first, second))

    tile = depth // 2
    here = lambda chip_, core_, half: (chip_ * 2 + core_) * 2 + half
    rows, sides = [], []
    for core_ in (1 - core, core):
        for chip_, side in ((chip, 0), (chip, 1), (1 - chip, 0)):
            for half in range(2):
                rows.append(here(chip_, core_, half))
                sides.append(side)
    rows = jnp.stack(rows).astype(jnp.int32)
    side = jnp.array(sides, jnp.int32)
    from_x = jnp.where(side == 0, chip == 0, chip != 0)
    def held(own):
        out = []
        following = rows[0]
        for t in range(len(sides) - 1, -1, -1):
            following = jnp.where(own[t], rows[t], following)
            out.append(following)
        return jnp.stack(out[::-1])
    table = jnp.stack([held(from_x), held(jnp.logical_not(from_x)), side])
    prod = products(table, pos, x, y, keep, send, tile)
    give, stay = prod[: 3 * depth], prod[3 * depth :]
    got = lax.ppermute(give, "slab", to_core)
    cut = lambda t: (stay[t * depth : (t + 1) * depth], got[t * depth : (t + 1) * depth])

    main, main_give, side_, side_give = pairings(
        halves, 0.5, pos, "pair_near", (keep, *cut(0)), (send, *cut(1))
    )
    side_sum = side_ + lax.ppermute(side_give, "slab", to_core)
    early = lax.ppermute(side_sum, "slab", to_chip)
    main_sum = main + lax.ppermute(main_give, "slab", to_core)
    cross, cross_give = pairings(halves, 1.0, pos, "pair_far", (far, *cut(2)))
    total = main_sum + early + (cross + lax.ppermute(cross_give, "slab", to_core))
    schur = total * lax.ppermute(total, "slab", to_chip)
    other = lax.ppermute(schur, "slab", to_core)
    own = pl.pallas_call(
        functools.partial(factor_kernel, halves),
        out_shape=jax.ShapeDtypeStruct((size // slabs, size), F32),
        in_specs=[SMEM, VMEM, VMEM],
        out_specs=VMEM,
        scratch_shapes=[pltpu.VMEM((size, size), F32)],
        name="factor",
    )(pos, schur, other)
    return place(own, dest, groups)


def any_chips(x, y, v, first, second, order, dest):
    slabs, groups = lax.axis_size("slab"), lax.axis_size("blk")
    size = first.shape[0]
    share = size // slabs
    slab = lax.axis_index("slab")
    row_start = slab * share

    def pairing(z, index):
        picked = select_columns(v, index)
        every = lax.all_gather(picked, "slab", axis=0, tiled=True)
        c = lax.dot_general(every, z, TN, preferred_element_type=F32).astype(BF16)
        return jnp.dot(c, picked, preferred_element_type=F32)

    both = jnp.concatenate([pairing(x, first), pairing(y, second)], axis=1)
    both = lax.psum_scatter(both, "slab", scatter_dimension=0, tiled=True)
    schur = both[:, :size] * both[:, size:]
    row_ids = row_start + jnp.arange(share, dtype=jnp.int32)
    col_ids = jnp.arange(size, dtype=jnp.int32)
    mask = (row_ids[:, None] < order) & (col_ids[None, :] < order)
    schur = jnp.where(mask, schur, 0.0) + (row_ids[:, None] == col_ids[None, :]).astype(F32)
    whole = lax.all_gather(schur, "slab", axis=0, tiled=True)
    whole = 0.5 * (whole + whole.T)
    pos = jnp.stack([slab // 2, slab % 2, row_start, order]).astype(jnp.int32)
    own = pl.pallas_call(
        factor_whole_kernel,
        out_shape=jax.ShapeDtypeStruct((share, size), F32),
        in_specs=[SMEM, VMEM],
        out_specs=VMEM,
        scratch_shapes=[pltpu.VMEM((size, size), F32)],
        name="factor",
    )(pos, whole)
    return place(own, dest, groups)


def on_device(xinv, ymat, basis, pair_index, orders, dest):
    order = orders[lax.axis_index("blk")]
    body = two_chips if lax.axis_size("slab") == 4 else any_chips
    return body(xinv[0], ymat[0], basis[0], pair_index[0, 0], pair_index[0, 1], order, dest)[None]


def solution(mesh):
    return jax.shard_map(
        on_device,
        mesh=mesh,
        in_specs=(
            P("blk", None, "slab"),
            P("blk", None, "slab"),
            P("blk", "slab", None),
            P("blk", None, None),
            P(),
            P(),
        ),
        out_specs=P("blk", "slab", None),
        check_vma=False,
    )
```

```python
import functools

import jax
import jax.numpy as jnp
from jax import lax
from jax.experimental import pallas as pl
from jax.experimental.pallas import tpu as pltpu
from jax.sharding import PartitionSpec as P


F32 = jnp.float32
BF16 = jnp.bfloat16
LANES = 128
MICRO = 8
VMEM = pl.BlockSpec(memory_space=pltpu.VMEM)
SMEM = pl.BlockSpec(memory_space=pltpu.SMEM)
TN = (((0,), (0,)), ((), ()))


def dot_f32(a, b, dims):
    dot = functools.partial(lax.dot_general, dimension_numbers=dims, preferred_element_type=F32)
    a_hi, b_hi = a.astype(BF16), b.astype(BF16)
    a_lo = (a - a_hi.astype(F32)).astype(BF16)
    b_lo = (b - b_hi.astype(F32)).astype(BF16)
    return dot(a_hi, b_hi) + (dot(a_hi, b_lo) + dot(a_lo, b_hi))


def lane_splat(x, lane):
    return jnp.broadcast_to(x[:, lane : lane + 1], (MICRO, LANES))


def row_splat(x, row):
    return jnp.broadcast_to(x[row : row + 1, :], (MICRO, x.shape[1]))


def by_tile(f, *wide):
    tiles = [f(*[x[:, t : t + LANES] for x in wide]) for t in range(0, wide[0].shape[1], LANES)]
    return tiles[0] if len(tiles) == 1 else jnp.concatenate(tiles, axis=1)


def factor_rows(a_ref, start, width):
    for m in range(0, LANES, MICRO):
        rows = a_ref[start + m : start + m + MICRO, start : start + width]
        cols = [lane_splat(rows[:, :LANES], m + k) for k in range(MICRO)]
        low = {(i, k): row_splat(cols[k], i) for k in range(MICRO) for i in range(k, MICRO)}
        inv = []
        for k in range(MICRO):
            inv.append(lax.rsqrt(low[k, k]))
            for i in range(k + 1, MICRO):
                low[i, k] = low[i, k] * inv[k]
            for j in range(k + 1, MICRO):
                for i in range(j, MICRO):
                    low[i, j] = low[i, j] - low[i, k] * low[j, k]
        wide = [row_splat(rows, i) for i in range(MICRO)]
        for k in range(MICRO):
            wide[k] = by_tile(lambda x: x * inv[k], wide[k])
            for i in range(k + 1, MICRO):
                wide[i] = by_tile(lambda x, u: x - low[i, k] * u, wide[i], wide[k])
        sub = lax.broadcasted_iota(jnp.int32, (MICRO, width), 0)
        lane = lax.broadcasted_iota(jnp.int32, (MICRO, width), 1)
        packed = wide[0]
        for k in range(1, MICRO):
            packed = jnp.where(sub == k, wide[k], packed)
        a_ref[start + m : start + m + MICRO, start : start + width] = jnp.where(lane >= sub + m, packed, 0.0)
        for later in range(m + MICRO, LANES, MICRO):
            here = pl.ds(start + later, MICRO)
            rest = a_ref[here, start : start + width]
            part = [lane_splat(rest[:, :LANES], m + k) for k in range(MICRO)]
            for k in range(MICRO):
                for j in range(k):
                    part[k] = part[k] - low[k, j] * part[j]
                part[k] = part[k] * inv[k]
            for k in range(MICRO):
                rest = by_tile(lambda x, u: x - part[k] * u, rest, wide[k])
            a_ref[here, start : start + width] = rest


def factor_all(a_ref):
    size = a_ref.shape[0]
    for start in range(0, size, LANES):
        factor_rows(a_ref, start, size - start)
        for row in range(start + LANES, size, LANES):
            left = a_ref[start : start + LANES, row : row + LANES]
            right = a_ref[start : start + LANES, row:]
            a_ref[row : row + LANES, row:] = a_ref[row : row + LANES, row:] - dot_f32(left, right, TN)


def own_rows(a_ref, out_ref, row_start):
    share, size = out_ref.shape
    base = pl.multiple_of(row_start // LANES * LANES, LANES)
    inner = row_start - base
    for q in range(0, size, LANES):
        block = a_ref[q : q + LANES, pl.ds(base, LANES)]
        block = jnp.where(q <= base, block, 0.0).T
        if share % LANES:
            keep = (
                lax.broadcasted_iota(jnp.int32, (share, LANES), 0) + inner
                == lax.broadcasted_iota(jnp.int32, (share, LANES), 1)
            ).astype(F32)
            block = lax.dot_general(
                keep, block, (((1,), (0,)), ((), ())),
                precision=lax.Precision.HIGHEST, preferred_element_type=F32,
            )
        out_ref[:, q : q + LANES] = block


def assemble(block, row, col, order):
    rows = lax.broadcasted_iota(jnp.int32, block.shape, 0) + row
    cols = lax.broadcasted_iota(jnp.int32, block.shape, 1) + col
    return jnp.where((rows < order) & (cols < order), block, 0.0) + (rows == cols).astype(F32)


def upper_blocks(size):
    count = size // LANES
    blocks = [(i, k) for k in range(count) for i in range(k + 1)]
    return blocks[: len(blocks) // 2], blocks[len(blocks) // 2 :]


def position():
    slab = lax.axis_index("slab")
    return slab // 2, slab % 2


def factor_kernel(halves, orders_ref, mine_ref, theirs_ref, out_ref, a_ref):
    _, core = position()
    order = orders_ref[lax.axis_index("blk")]
    for turn in range(2):
        @pl.when(core == turn)
        def _():
            for ref, half in ((mine_ref, halves[turn]), (theirs_ref, halves[1 - turn])):
                for t, (i, k) in enumerate(half):
                    i, k = i * LANES, k * LANES
                    a_ref[i : i + LANES, k : k + LANES] = assemble(ref[t], i, k, order)
    factor_all(a_ref)
    own_rows(a_ref, out_ref, lax.axis_index("slab") * out_ref.shape[0])


def factor_whole_kernel(s_ref, out_ref, a_ref):
    a_ref[...] = s_ref[...]
    factor_all(a_ref)
    own_rows(a_ref, out_ref, lax.axis_index("slab") * out_ref.shape[0])


def one_hot(index, rows):
    return (lax.broadcasted_iota(jnp.int32, (rows, index.shape[1]), 0) == index).astype(F32).astype(BF16)


def select_send_kernel(index_ref, v_ref, send_ref):
    chip, _ = position()
    index = jnp.where(chip == 0, index_ref[1:2], index_ref[0:1])
    send_ref[...] = jnp.dot(v_ref[...], one_hot(index, v_ref.shape[1]), preferred_element_type=F32).astype(BF16)


def select_keep_kernel(index_ref, v_ref, send_ref, keep_ref, pay_ref):
    chip, core = position()
    index = jnp.where(chip == 0, index_ref[0:1], index_ref[1:2])
    keep_ref[...] = jnp.dot(v_ref[...], one_hot(index, v_ref.shape[1]), preferred_element_type=F32).astype(BF16)

    @pl.when(core == 0)
    def _():
        pay_ref[...] = send_ref[...]

    @pl.when(core == 1)
    def _():
        pay_ref[...] = keep_ref[...]


def split_upper(total_ref, halves, core, base, mine_ref, give_ref):
    for turn in range(2):
        @pl.when(core == turn)
        def _():
            for ref, half in ((mine_ref, halves[turn]), (give_ref, halves[1 - turn])):
                for t, (i, k) in enumerate(half):
                    i, k = i * LANES, k * LANES
                    mirror = total_ref[k : k + LANES, i : i + LANES].T
                    ref[base + t] = total_ref[i : i + LANES, k : k + LANES] + mirror


def near_unit(step):
    return step // 2


def near_kernel(halves, x_ref, y_ref, keep_ref, send_ref, cross_ref, mine_ref, give_ref, main_ref, side_ref):
    step = pl.program_id(0)
    chip, core = position()
    unit = near_unit(step)
    tile = x_ref.shape[0]
    rows = pl.ds((step % 2) * tile, tile)
    is_main = (unit == 0) | ((unit == 2) & (core == 0))

    @pl.when(step == 0)
    def _():
        main_ref[...] = jnp.zeros_like(main_ref)
        side_ref[...] = jnp.zeros_like(side_ref)

    def add(z_ref, sel_ref, left_ref, scale, total_ref):
        u = jnp.dot(z_ref[...], sel_ref[...], preferred_element_type=F32)
        u = (u * scale).astype(BF16)
        total_ref[...] += lax.dot_general(left_ref[rows, :], u, TN, preferred_element_type=F32)

    for main_side, sel_ref, total_ref in ((True, keep_ref, main_ref), (False, send_ref, side_ref)):
        for here in range(2):
            z_ref = x_ref if (here == 0) == main_side else y_ref
            at = (is_main == main_side) & (chip == here)
            pl.when(at & (unit != 2))(lambda: add(z_ref, sel_ref, sel_ref, 0.5, total_ref))
            pl.when(at & (unit == 2))(lambda: add(z_ref, sel_ref, cross_ref, 1.0, total_ref))

    @pl.when(step == pl.num_programs(0) - 1)
    def _():
        half = len(halves[0])
        split_upper(side_ref, halves, core, 0, mine_ref, give_ref)
        split_upper(main_ref, halves, core, half, mine_ref, give_ref)


def near(halves, x, y, keep, send, cross):
    depth, size = keep.shape
    tile = depth // 2

    def reads(matrix):
        def index(step):
            chip, core = position()
            unit = near_unit(step)
            is_main = (unit == 0) | ((unit == 2) & (core == 0))
            mine = is_main == (chip == matrix)
            own, other = (chip * 2 + core) * 2, (chip * 2 + 1 - core) * 2
            late = jnp.where((core == 0) == (chip == matrix), other, own + 1)
            early = jnp.where(chip == matrix, own, own)
            row = jnp.where(unit == 2, other, own) + step % 2
            after = jnp.where(step >= 2, late, early)
            return jnp.where(mine, row, after), 0

        return index

    whole = lambda step: (0, 0)
    blocks = (2 * len(halves[0]), LANES, LANES)
    return pl.pallas_call(
        functools.partial(near_kernel, halves),
        out_shape=(jax.ShapeDtypeStruct(blocks, F32), jax.ShapeDtypeStruct(blocks, F32)),
        grid=(6,),
        in_specs=[
            pl.BlockSpec((tile, depth), reads(0)),
            pl.BlockSpec((tile, depth), reads(1)),
            pl.BlockSpec(keep.shape, whole),
            pl.BlockSpec(keep.shape, whole),
            pl.BlockSpec(keep.shape, whole),
        ],
        out_specs=(
            pl.BlockSpec(blocks, lambda step: (0, 0, 0)),
            pl.BlockSpec(blocks, lambda step: (0, 0, 0)),
        ),
        scratch_shapes=[pltpu.VMEM((size, size), F32), pltpu.VMEM((size, size), F32)],
        cost_estimate=pl.CostEstimate(
            flops=6 * depth * size * (depth + size), bytes_accessed=6 * depth * (depth + size), transcendentals=0
        ),
        name="near",
    )(x, y, keep, send, cross)


def far_products_kernel(x_ref, y_ref, keep_ref, give_ref, stay_ref):
    chip, _ = position()
    step = pl.program_id(0)
    for here, z_ref in ((0, x_ref), (1, y_ref)):
        for turn, out_ref in ((0, give_ref), (1, stay_ref)):
            @pl.when((chip == here) & (step // 2 == turn))
            def _():
                out_ref[...] = jnp.dot(z_ref[...], keep_ref[...], preferred_element_type=F32).astype(BF16)


def far_products(x, y, keep):
    depth, size = keep.shape
    tile = depth // 2

    def reads(matrix):
        def index(step):
            chip, core = position()
            holder = jnp.where(step < 2, 1 - core, core)
            row = ((1 - chip) * 2 + holder) * 2 + step % 2
            return jnp.where(chip == matrix, row, 0), 0

        return index

    return pl.pallas_call(
        far_products_kernel,
        out_shape=(jax.ShapeDtypeStruct(keep.shape, BF16), jax.ShapeDtypeStruct(keep.shape, BF16)),
        grid=(4,),
        in_specs=[
            pl.BlockSpec((tile, depth), reads(0)),
            pl.BlockSpec((tile, depth), reads(1)),
            pl.BlockSpec(keep.shape, lambda step: (0, 0)),
        ],
        out_specs=(
            pl.BlockSpec((tile, size), lambda step: (jnp.minimum(step, 1), 0)),
            pl.BlockSpec((tile, size), lambda step: (jnp.maximum(step - 2, 0), 0)),
        ),
        cost_estimate=pl.CostEstimate(
            flops=4 * depth * depth * size, bytes_accessed=4 * depth * (depth + size), transcendentals=0
        ),
        name="far_products",
    )(x, y, keep)


def far_kernel(halves, sel_ref, own_ref, other_ref, mine_ref, give_ref, total_ref):
    _, core = position()
    both = (own_ref[...].astype(F32) + other_ref[...].astype(F32)).astype(BF16)
    total_ref[...] = lax.dot_general(sel_ref[...], both, TN, preferred_element_type=F32)
    split_upper(total_ref, halves, core, 0, mine_ref, give_ref)


def select_columns(v, index):
    hot = (lax.broadcasted_iota(jnp.int32, (v.shape[1], index.shape[0]), 0) == index[None, :]).astype(BF16)
    return jnp.dot(v, hot, preferred_element_type=F32).astype(BF16)


def place(own, dest, groups):
    source = jnp.argmax(dest[None, :] == jnp.arange(groups, dtype=dest.dtype)[:, None], axis=1)
    pieces = own.reshape(groups, own.shape[0] // groups, own.shape[1])
    pieces = lax.all_to_all(pieces, "blk", 0, 0)
    pieces = jnp.take(pieces, source, axis=0)
    pieces = lax.all_to_all(pieces, "blk", 0, 0)
    return pieces.reshape(own.shape)


def two_chips(x, y, v, index, orders, dest):
    slabs, groups = lax.axis_size("slab"), lax.axis_size("blk")
    depth, size = v.shape[0], index.shape[1]
    halves = upper_blocks(size)
    half = len(halves[0])
    to_core = [(s, s ^ 1) for s in range(slabs)]
    to_chip = [(s, s ^ 2) for s in range(slabs)]
    picked = jax.ShapeDtypeStruct((depth, size), BF16)
    blocks = jax.ShapeDtypeStruct((half, LANES, LANES), F32)

    send = pl.pallas_call(
        select_send_kernel, out_shape=picked, in_specs=[VMEM] * 2, out_specs=VMEM, name="select_send"
    )(index, v)
    far = lax.ppermute(send, "slab", to_chip)
    keep, pay = pl.pallas_call(
        select_keep_kernel, out_shape=(picked, picked), in_specs=[VMEM] * 3, out_specs=(VMEM, VMEM),
        name="select_keep",
    )(index, v, send)
    cross = lax.ppermute(pay, "slab", to_core)
    mine, give = near(halves, x, y, keep, send, cross)
    got = lax.ppermute(give, "slab", to_core)
    far_give, far_stay = far_products(x, y, keep)
    far_got = lax.ppermute(far_give, "slab", to_core)
    side_sum = mine[:half] + got[:half]
    early = lax.ppermute(side_sum, "slab", to_chip)
    far_mine, far_give = pl.pallas_call(
        functools.partial(far_kernel, halves),
        out_shape=(blocks, blocks),
        in_specs=[VMEM] * 3,
        out_specs=(VMEM, VMEM),
        scratch_shapes=[pltpu.VMEM((size, size), F32)],
        cost_estimate=pl.CostEstimate(
            flops=2 * depth * size * size, bytes_accessed=6 * depth * size, transcendentals=0
        ),
        name="far",
    )(far, far_stay, far_got)
    total = (mine[half:] + got[half:]) + early + (far_mine + lax.ppermute(far_give, "slab", to_core))
    schur = total * lax.ppermute(total, "slab", to_chip)
    other = lax.ppermute(schur, "slab", to_core)
    own = pl.pallas_call(
        functools.partial(factor_kernel, halves),
        out_shape=jax.ShapeDtypeStruct((size // slabs, size), F32),
        in_specs=[SMEM, VMEM, VMEM],
        out_specs=VMEM,
        scratch_shapes=[pltpu.VMEM((size, size), F32)],
        name="factor",
    )(orders, schur, other)
    return place(own, dest, groups)


def any_chips(x, y, v, index, orders, dest):
    slabs, groups = lax.axis_size("slab"), lax.axis_size("blk")
    first, second = index
    order = orders[lax.axis_index("blk")]
    size = first.shape[0]
    share = size // slabs
    slab = lax.axis_index("slab")
    row_start = slab * share

    def pairing(z, index):
        picked = select_columns(v, index)
        every = lax.all_gather(picked, "slab", axis=0, tiled=True)
        c = lax.dot_general(every, z, TN, preferred_element_type=F32).astype(BF16)
        return jnp.dot(c, picked, preferred_element_type=F32)

    both = jnp.concatenate([pairing(x, first), pairing(y, second)], axis=1)
    both = lax.psum_scatter(both, "slab", scatter_dimension=0, tiled=True)
    schur = both[:, :size] * both[:, size:]
    row_ids = row_start + jnp.arange(share, dtype=jnp.int32)
    col_ids = jnp.arange(size, dtype=jnp.int32)
    mask = (row_ids[:, None] < order) & (col_ids[None, :] < order)
    schur = jnp.where(mask, schur, 0.0) + (row_ids[:, None] == col_ids[None, :]).astype(F32)
    whole = lax.all_gather(schur, "slab", axis=0, tiled=True)
    whole = 0.5 * (whole + whole.T)
    own = pl.pallas_call(
        factor_whole_kernel,
        out_shape=jax.ShapeDtypeStruct((share, size), F32),
        in_specs=[VMEM],
        out_specs=VMEM,
        scratch_shapes=[pltpu.VMEM((size, size), F32)],
        name="factor",
    )(whole)
    return place(own, dest, groups)


def on_device(xinv, ymat, basis, pair_index, orders, dest):
    body = two_chips if lax.axis_size("slab") == 4 else any_chips
    return body(xinv[0], ymat[0], basis[0], pair_index[0], orders, dest)[None]


def solution(mesh):
    return jax.shard_map(
        on_device,
        mesh=mesh,
        in_specs=(
            P("blk", None, "slab"),
            P("blk", None, "slab"),
            P("blk", "slab", None),
            P("blk", None, None),
            P(),
            P(),
        ),
        out_specs=P("blk", "slab", None),
        check_vma=False,
    )
```

```python
import functools

import jax
import jax.numpy as jnp
from jax import lax
from jax.experimental import pallas as pl
from jax.experimental.pallas import tpu as pltpu
from jax.sharding import PartitionSpec as P


F32 = jnp.float32
BF16 = jnp.bfloat16
LANES = 128
MICRO = 8
GROUP = 4
VMEM = pl.BlockSpec(memory_space=pltpu.VMEM)
SMEM = pl.BlockSpec(memory_space=pltpu.SMEM)
TN = (((0,), (0,)), ((), ()))


def dot_f32(a, b, dims):
    dot = functools.partial(lax.dot_general, dimension_numbers=dims, preferred_element_type=F32)
    a_hi, b_hi = a.astype(BF16), b.astype(BF16)
    a_lo = (a - a_hi.astype(F32)).astype(BF16)
    b_lo = (b - b_hi.astype(F32)).astype(BF16)
    return dot(a_hi, b_hi) + (dot(a_hi, b_lo) + dot(a_lo, b_hi))


def lane_splat(x, lane):
    return jnp.take_along_axis(x, jnp.full((MICRO, LANES), lane, jnp.int32), axis=1)


def row_splat(x, row):
    return jnp.broadcast_to(x[row : row + 1, :], (MICRO, x.shape[1]))


def by_tile(f, *wide):
    tiles = [f(*[x[:, t : t + LANES] for x in wide]) for t in range(0, wide[0].shape[1], LANES)]
    return tiles[0] if len(tiles) == 1 else jnp.concatenate(tiles, axis=1)


def factor_rows(a_ref, start, width):
    cols = None
    span = slice(start, start + width)
    count = LANES // MICRO
    for m in range(count):
        base = MICRO * m
        here = slice(start + base, start + base + MICRO)
        rows = a_ref[here, span]
        if cols is None:
            cols = [lane_splat(rows[:, :LANES], base + k) for k in range(MICRO)]
        low = {(i, k): row_splat(cols[k], i) for k in range(MICRO) for i in range(k, MICRO)}
        inv = []
        for k in range(MICRO):
            inv.append(lax.rsqrt(low[k, k]))
            for i in range(k + 1, MICRO):
                low[i, k] = low[i, k] * inv[k]
            for j in range(k + 1, MICRO):
                for i in range(j, MICRO):
                    low[i, j] = low[i, j] - low[i, k] * low[j, k]
        wide = [row_splat(rows, i) for i in range(MICRO)]
        for k in range(MICRO):
            wide[k] = by_tile(lambda x: x * inv[k], wide[k])
            for i in range(k + 1, MICRO):
                wide[i] = by_tile(lambda x, u: x - low[i, k] * u, wide[i], wide[k])
        sub = lax.broadcasted_iota(jnp.int32, (MICRO, width), 0)
        lane = lax.broadcasted_iota(jnp.int32, (MICRO, width), 1)
        packed = wide[0]
        for k in range(1, MICRO):
            packed = jnp.where(sub == k, wide[k], packed)
        a_ref[here, span] = jnp.where(lane >= sub + base, packed, 0.0)
        group_end = (m // GROUP + 1) * GROUP
        cols = None
        for later in range(m + 1, min(group_end + 1, count)):
            there = slice(start + MICRO * later, start + MICRO * later + MICRO)
            rest = a_ref[there, span]
            head = rest[:, :LANES]
            part = [lane_splat(head, base + k) for k in range(MICRO)]
            for k in range(MICRO):
                for j in range(k):
                    part[k] = part[k] - low[k, j] * part[j]
                part[k] = part[k] * inv[k]
            if later == m + 1:
                cols = [lane_splat(head, MICRO * later + j) for j in range(MICRO)]
                for k in range(MICRO):
                    for j in range(MICRO):
                        cols[j] = cols[j] - part[k] * row_splat(part[k], j)
            for k in range(MICRO):
                rest = by_tile(lambda x, u: x - part[k] * u, rest, wide[k])
            a_ref[there, span] = rest
        if m + 1 == group_end and group_end + 1 < count:
            done = a_ref[start + MICRO * (group_end - GROUP) : start + MICRO * group_end, span]
            first = MICRO * (group_end + 1)
            there = slice(start + first, start + LANES)
            a_ref[there, span] = a_ref[there, span] - dot_f32(done[:, :LANES], done, TN)[first:]


def factor_all(a_ref):
    size = a_ref.shape[0]
    for start in range(0, size, LANES):
        factor_rows(a_ref, start, size - start)
        for row in range(start + LANES, size, LANES):
            left = a_ref[start : start + LANES, row : row + LANES]
            right = a_ref[start : start + LANES, row:]
            a_ref[row : row + LANES, row:] = a_ref[row : row + LANES, row:] - dot_f32(left, right, TN)


def own_rows(a_ref, out_ref, row_start):
    share, size = out_ref.shape
    base = pl.multiple_of(row_start // LANES * LANES, LANES)
    inner = row_start - base
    for q in range(0, size, LANES):
        block = a_ref[q : q + LANES, pl.ds(base, LANES)]
        block = jnp.where(q <= base, block, 0.0).T
        if share % LANES:
            keep = (
                lax.broadcasted_iota(jnp.int32, (share, LANES), 0) + inner
                == lax.broadcasted_iota(jnp.int32, (share, LANES), 1)
            ).astype(F32)
            block = lax.dot_general(
                keep, block, (((1,), (0,)), ((), ())),
                precision=lax.Precision.HIGHEST, preferred_element_type=F32,
            )
        out_ref[:, q : q + LANES] = block


def assemble(block, row, col, order):
    rows = lax.broadcasted_iota(jnp.int32, block.shape, 0) + row
    cols = lax.broadcasted_iota(jnp.int32, block.shape, 1) + col
    return jnp.where((rows < order) & (cols < order), block, 0.0) + (rows == cols).astype(F32)


def upper_blocks(size):
    count = size // LANES
    blocks = [(i, k) for k in range(count) for i in range(k + 1)]
    return blocks[: len(blocks) // 2], blocks[len(blocks) // 2 :]


def position():
    slab = lax.axis_index("slab")
    return slab // 2, slab % 2


def factor_kernel(halves, orders_ref, mine_ref, theirs_ref, out_ref, a_ref):
    _, core = position()
    order = orders_ref[lax.axis_index("blk")]
    for turn in range(2):
        @pl.when(core == turn)
        def _():
            for ref, half in ((mine_ref, halves[turn]), (theirs_ref, halves[1 - turn])):
                for t, (i, k) in enumerate(half):
                    i, k = i * LANES, k * LANES
                    a_ref[i : i + LANES, k : k + LANES] = assemble(ref[t], i, k, order)
    factor_all(a_ref)
    own_rows(a_ref, out_ref, lax.axis_index("slab") * out_ref.shape[0])


def factor_whole_kernel(s_ref, out_ref, a_ref):
    a_ref[...] = s_ref[...]
    factor_all(a_ref)
    own_rows(a_ref, out_ref, lax.axis_index("slab") * out_ref.shape[0])


def split_upper(total_ref, halves, core, base, mine_ref, give_ref):
    for turn in range(2):
        @pl.when(core == turn)
        def _():
            for ref, half in ((mine_ref, halves[turn]), (give_ref, halves[1 - turn])):
                for t, (i, k) in enumerate(half):
                    i, k = i * LANES, k * LANES
                    mirror = total_ref[k : k + LANES, i : i + LANES].T
                    ref[base + t] = total_ref[i : i + LANES, k : k + LANES] + mirror


def near_unit(step):
    return step // 2


def near_kernel(
    halves, x_ref, y_ref, keep_ref, send_ref, keep_got_ref, send_got_ref, mine_ref, give_ref, main_ref, side_ref
):
    step = pl.program_id(0)
    chip, core = position()
    unit = near_unit(step)
    tile = x_ref.shape[0]
    rows = pl.ds((step % 2) * tile, tile)
    is_main = (unit == 0) | ((unit == 2) & (core == 0))

    @pl.when(step == 0)
    def _():
        main_ref[...] = jnp.zeros_like(main_ref)
        side_ref[...] = jnp.zeros_like(side_ref)

    def add(z_ref, sel_ref, left_ref, scale, total_ref):
        u = jnp.dot(z_ref[...], sel_ref[...], preferred_element_type=F32)
        u = (u * scale).astype(BF16)
        total_ref[...] += lax.dot_general(left_ref[rows, :], u, TN, preferred_element_type=F32)

    for main_side, sel_ref, cross_ref, total_ref in (
        (True, keep_ref, keep_got_ref, main_ref),
        (False, send_ref, send_got_ref, side_ref),
    ):
        for here in range(2):
            z_ref = x_ref if (here == 0) == main_side else y_ref
            at = (is_main == main_side) & (chip == here)
            pl.when(at & (unit != 2))(lambda: add(z_ref, sel_ref, sel_ref, 0.5, total_ref))
            pl.when(at & (unit == 2))(lambda: add(z_ref, sel_ref, cross_ref, 1.0, total_ref))

    @pl.when(step == pl.num_programs(0) - 1)
    def _():
        half = len(halves[0])
        split_upper(side_ref, halves, core, 0, mine_ref, give_ref)
        split_upper(main_ref, halves, core, half, mine_ref, give_ref)


def near(halves, x, y, keep, send, keep_got, send_got):
    depth, size = keep.shape
    tile = depth // 2

    def reads(matrix):
        def index(step):
            chip, core = position()
            unit = near_unit(step)
            is_main = (unit == 0) | ((unit == 2) & (core == 0))
            mine = is_main == (chip == matrix)
            own, other = (chip * 2 + core) * 2, (chip * 2 + 1 - core) * 2
            late = jnp.where((core == 0) == (chip == matrix), other, own + 1)
            early = jnp.where(chip == matrix, own, own)
            row = jnp.where(unit == 2, other, own) + step % 2
            after = jnp.where(step >= 2, late, early)
            return jnp.where(mine, row, after), 0

        return index

    whole = lambda step: (0, 0)
    blocks = (2 * len(halves[0]), LANES, LANES)
    return pl.pallas_call(
        functools.partial(near_kernel, halves),
        out_shape=(jax.ShapeDtypeStruct(blocks, F32), jax.ShapeDtypeStruct(blocks, F32)),
        grid=(6,),
        in_specs=[
            pl.BlockSpec((tile, depth), reads(0)),
            pl.BlockSpec((tile, depth), reads(1)),
        ]
        + [pl.BlockSpec(keep.shape, whole)] * 4,
        out_specs=(
            pl.BlockSpec(blocks, lambda step: (0, 0, 0)),
            pl.BlockSpec(blocks, lambda step: (0, 0, 0)),
        ),
        scratch_shapes=[pltpu.VMEM((size, size), F32), pltpu.VMEM((size, size), F32)],
        cost_estimate=pl.CostEstimate(
            flops=6 * depth * size * (depth + size), bytes_accessed=6 * depth * (depth + size), transcendentals=0
        ),
        name="near",
    )(x, y, keep, send, keep_got, send_got)


def far_products_kernel(x_ref, y_ref, keep_ref, give_ref, stay_ref):
    chip, _ = position()
    step = pl.program_id(0)
    for here, z_ref in ((0, x_ref), (1, y_ref)):
        for turn, out_ref in ((0, give_ref), (1, stay_ref)):
            @pl.when((chip == here) & (step // 2 == turn))
            def _():
                out_ref[...] = jnp.dot(z_ref[...], keep_ref[...], preferred_element_type=F32).astype(BF16)


def far_products(x, y, keep):
    depth, size = keep.shape
    tile = depth // 2

    def reads(matrix):
        def index(step):
            chip, core = position()
            holder = jnp.where(step < 2, 1 - core, core)
            row = ((1 - chip) * 2 + holder) * 2 + step % 2
            return jnp.where(chip == matrix, row, 0), 0

        return index

    return pl.pallas_call(
        far_products_kernel,
        out_shape=(jax.ShapeDtypeStruct(keep.shape, BF16), jax.ShapeDtypeStruct(keep.shape, BF16)),
        grid=(4,),
        in_specs=[
            pl.BlockSpec((tile, depth), reads(0)),
            pl.BlockSpec((tile, depth), reads(1)),
            pl.BlockSpec(keep.shape, lambda step: (0, 0)),
        ],
        out_specs=(
            pl.BlockSpec((tile, size), lambda step: (jnp.minimum(step, 1), 0)),
            pl.BlockSpec((tile, size), lambda step: (jnp.maximum(step - 2, 0), 0)),
        ),
        cost_estimate=pl.CostEstimate(
            flops=4 * depth * depth * size, bytes_accessed=4 * depth * (depth + size), transcendentals=0
        ),
        name="far_products",
    )(x, y, keep)


def far_kernel(halves, sel_ref, both_ref, mine_ref, give_ref, total_ref):
    _, core = position()
    total_ref[...] = lax.dot_general(sel_ref[...], both_ref[...], TN, preferred_element_type=F32)
    split_upper(total_ref, halves, core, 0, mine_ref, give_ref)


def select_columns(v, index):
    hot = (lax.broadcasted_iota(jnp.int32, (v.shape[1], index.shape[0]), 0) == index[None, :]).astype(BF16)
    return jnp.dot(v, hot, preferred_element_type=F32).astype(BF16)


def place(own, dest, groups):
    source = jnp.argmax(dest[None, :] == jnp.arange(groups, dtype=dest.dtype)[:, None], axis=1)
    pieces = own.reshape(groups, own.shape[0] // groups, own.shape[1])
    pieces = lax.all_to_all(pieces, "blk", 0, 0)
    pieces = jnp.take(pieces, source, axis=0)
    pieces = lax.all_to_all(pieces, "blk", 0, 0)
    return pieces.reshape(own.shape)


def two_chips(x, y, v, index, orders, dest):
    slabs, groups = lax.axis_size("slab"), lax.axis_size("blk")
    depth, size = v.shape[0], index.shape[1]
    halves = upper_blocks(size)
    half = len(halves[0])
    to_core = [(s, s ^ 1) for s in range(slabs)]
    to_chip = [(s, s ^ 2) for s in range(slabs)]
    blocks = jax.ShapeDtypeStruct((half, LANES, LANES), F32)
    chip, _ = position()
    first, second = index

    send = select_columns(v, jnp.where(chip == 0, second, first))
    far = lax.ppermute(send, "slab", to_chip)
    send_got = lax.ppermute(send, "slab", [(s, d) for s, d in to_core if s < d])
    keep = select_columns(v, jnp.where(chip == 0, first, second))
    keep_got = lax.ppermute(keep, "slab", [(s, d) for s, d in to_core if s > d])
    mine, give = near(halves, x, y, keep, send, keep_got, send_got)
    got = lax.ppermute(give, "slab", to_core)
    side_sum = mine[:half] + got[:half]
    early = lax.ppermute(side_sum, "slab", to_chip)
    far_give, far_stay = far_products(x, y, keep)
    far_got = lax.ppermute(far_give, "slab", to_core)
    both = (far_stay.astype(F32) + far_got.astype(F32)).astype(BF16)
    far_mine, far_give = pl.pallas_call(
        functools.partial(far_kernel, halves),
        out_shape=(blocks, blocks),
        in_specs=[VMEM] * 2,
        out_specs=(VMEM, VMEM),
        scratch_shapes=[pltpu.VMEM((size, size), F32)],
        cost_estimate=pl.CostEstimate(
            flops=2 * depth * size * size, bytes_accessed=4 * depth * size, transcendentals=0
        ),
        name="far",
    )(far, both)
    total = (mine[half:] + got[half:]) + early + (far_mine + lax.ppermute(far_give, "slab", to_core))
    schur = total * lax.ppermute(total, "slab", to_chip)
    other = lax.ppermute(schur, "slab", to_core)
    own = pl.pallas_call(
        functools.partial(factor_kernel, halves),
        out_shape=jax.ShapeDtypeStruct((size // slabs, size), F32),
        in_specs=[SMEM, VMEM, VMEM],
        out_specs=VMEM,
        scratch_shapes=[pltpu.VMEM((size, size), F32)],
        name="factor",
    )(orders, schur, other)
    return place(own, dest, groups)


def any_chips(x, y, v, index, orders, dest):
    slabs, groups = lax.axis_size("slab"), lax.axis_size("blk")
    first, second = index
    order = orders[lax.axis_index("blk")]
    size = first.shape[0]
    share = size // slabs
    slab = lax.axis_index("slab")
    row_start = slab * share

    def pairing(z, index):
        picked = select_columns(v, index)
        every = lax.all_gather(picked, "slab", axis=0, tiled=True)
        c = lax.dot_general(every, z, TN, preferred_element_type=F32).astype(BF16)
        return jnp.dot(c, picked, preferred_element_type=F32)

    both = jnp.concatenate([pairing(x, first), pairing(y, second)], axis=1)
    both = lax.psum_scatter(both, "slab", scatter_dimension=0, tiled=True)
    schur = both[:, :size] * both[:, size:]
    row_ids = row_start + jnp.arange(share, dtype=jnp.int32)
    col_ids = jnp.arange(size, dtype=jnp.int32)
    mask = (row_ids[:, None] < order) & (col_ids[None, :] < order)
    schur = jnp.where(mask, schur, 0.0) + (row_ids[:, None] == col_ids[None, :]).astype(F32)
    whole = lax.all_gather(schur, "slab", axis=0, tiled=True)
    whole = 0.5 * (whole + whole.T)
    own = pl.pallas_call(
        factor_whole_kernel,
        out_shape=jax.ShapeDtypeStruct((share, size), F32),
        in_specs=[VMEM],
        out_specs=VMEM,
        scratch_shapes=[pltpu.VMEM((size, size), F32)],
        name="factor",
    )(whole)
    return place(own, dest, groups)


def on_device(xinv, ymat, basis, pair_index, orders, dest):
    body = two_chips if lax.axis_size("slab") == 4 else any_chips
    return body(xinv[0], ymat[0], basis[0], pair_index[0], orders, dest)[None]


def solution(mesh):
    return jax.shard_map(
        on_device,
        mesh=mesh,
        in_specs=(
            P("blk", None, "slab"),
            P("blk", None, "slab"),
            P("blk", "slab", None),
            P("blk", None, None),
            P(),
            P(),
        ),
        out_specs=P("blk", "slab", None),
        check_vma=False,
    )
```

```python
import functools

import jax
import jax.numpy as jnp
from jax import lax
from jax.experimental import pallas as pl
from jax.experimental.pallas import tpu as pltpu
from jax.sharding import PartitionSpec as P


F32 = jnp.float32
BF16 = jnp.bfloat16
LANES = 128
MICRO = 8
GROUP = 4
AHEAD = 1
VMEM = pl.BlockSpec(memory_space=pltpu.VMEM)
SMEM = pl.BlockSpec(memory_space=pltpu.SMEM)
ANY = pl.BlockSpec(memory_space=pl.ANY)
TN = (((0,), (0,)), ((), ()))
NT = (((1,), (1,)), ((), ()))


def dot_f32(a, b, dims):
    dot = functools.partial(lax.dot_general, dimension_numbers=dims, preferred_element_type=F32)
    a_hi, b_hi = a.astype(BF16), b.astype(BF16)
    a_lo = (a - a_hi.astype(F32)).astype(BF16)
    b_lo = (b - b_hi.astype(F32)).astype(BF16)
    return dot(a_hi, b_hi) + (dot(a_hi, b_lo) + dot(a_lo, b_hi))


def lane_splat(x, lane):
    return jnp.take_along_axis(x, jnp.full((MICRO, LANES), lane, jnp.int32), axis=1)


def row_splat(x, row):
    return jnp.broadcast_to(x[row : row + 1, :], (MICRO, x.shape[1]))


def by_tile(f, *wide):
    tiles = [f(*[x[:, t : t + LANES] for x in wide]) for t in range(0, wide[0].shape[1], LANES)]
    return tiles[0] if len(tiles) == 1 else jnp.concatenate(tiles, axis=1)


def factor_rows(a_ref, start, width):
    cols = None
    span = slice(start, start + width)
    count = LANES // MICRO
    for m in range(count):
        base = MICRO * m
        here = slice(start + base, start + base + MICRO)
        rows = a_ref[here, span]
        if cols is None:
            cols = [lane_splat(rows[:, :LANES], base + k) for k in range(MICRO)]
        low = {(i, k): row_splat(cols[k], i) for k in range(MICRO) for i in range(k, MICRO)}
        inv = []
        for k in range(MICRO):
            inv.append(lax.rsqrt(low[k, k]))
            for i in range(k + 1, MICRO):
                low[i, k] = low[i, k] * inv[k]
            for j in range(k + 1, MICRO):
                for i in range(j, MICRO):
                    low[i, j] = low[i, j] - low[i, k] * low[j, k]
        wide = [row_splat(rows, i) for i in range(MICRO)]
        for k in range(MICRO):
            wide[k] = by_tile(lambda x: x * inv[k], wide[k])
            for i in range(k + 1, MICRO):
                wide[i] = by_tile(lambda x, u: x - low[i, k] * u, wide[i], wide[k])
        sub = lax.broadcasted_iota(jnp.int32, (MICRO, width), 0)
        lane = lax.broadcasted_iota(jnp.int32, (MICRO, width), 1)
        packed = wide[0]
        for k in range(1, MICRO):
            packed = jnp.where(sub == k, wide[k], packed)
        a_ref[here, span] = jnp.where(lane >= sub + base, packed, 0.0)
        group_end = (m // GROUP + 1) * GROUP
        cols = None
        for later in range(m + 1, min(group_end + AHEAD, count)):
            there = slice(start + MICRO * later, start + MICRO * later + MICRO)
            rest = a_ref[there, span]
            head = rest[:, :LANES]
            part = [lane_splat(head, base + k) for k in range(MICRO)]
            for k in range(MICRO):
                for j in range(k):
                    part[k] = part[k] - low[k, j] * part[j]
                part[k] = part[k] * inv[k]
            if later == m + 1:
                cols = [lane_splat(head, MICRO * later + j) for j in range(MICRO)]
                for k in range(MICRO):
                    for j in range(MICRO):
                        cols[j] = cols[j] - part[k] * row_splat(part[k], j)
            for k in range(MICRO):
                rest = by_tile(lambda x, u: x - part[k] * u, rest, wide[k])
            a_ref[there, span] = rest
        if m + 1 == group_end and group_end + AHEAD < count:
            done = a_ref[start + MICRO * (group_end - GROUP) : start + MICRO * group_end, span]
            first = MICRO * (group_end + AHEAD)
            there = slice(start + first, start + LANES)
            a_ref[there, span] = a_ref[there, span] - dot_f32(done[:, :LANES], done, TN)[first:]


def factor_all(a_ref):
    size = a_ref.shape[0]
    for start in range(0, size, LANES):
        factor_rows(a_ref, start, size - start)
        for row in range(start + LANES, size, LANES):
            left = a_ref[start : start + LANES, row : row + LANES]
            right = a_ref[start : start + LANES, row:]
            a_ref[row : row + LANES, row:] = a_ref[row : row + LANES, row:] - dot_f32(left, right, TN)


def own_rows(a_ref, out_ref, row_start):
    share, size = out_ref.shape
    base = pl.multiple_of(row_start // LANES * LANES, LANES)
    inner = row_start - base
    for q in range(0, size, LANES):
        block = a_ref[q : q + LANES, pl.ds(base, LANES)]
        block = jnp.where(q <= base, block, 0.0).T
        if share % LANES:
            keep = (
                lax.broadcasted_iota(jnp.int32, (share, LANES), 0) + inner
                == lax.broadcasted_iota(jnp.int32, (share, LANES), 1)
            ).astype(F32)
            block = lax.dot_general(
                keep, block, (((1,), (0,)), ((), ())),
                precision=lax.Precision.HIGHEST, preferred_element_type=F32,
            )
        out_ref[:, q : q + LANES] = block


def assemble(block, row, col, order):
    rows = lax.broadcasted_iota(jnp.int32, block.shape, 0) + row
    cols = lax.broadcasted_iota(jnp.int32, block.shape, 1) + col
    return jnp.where((rows < order) & (cols < order), block, 0.0) + (rows == cols).astype(F32)


def upper_blocks(size):
    count = size // LANES
    blocks = [(i, k) for k in range(count) for i in range(k + 1)]
    return blocks[: len(blocks) // 2], blocks[len(blocks) // 2 :]


def position():
    slab = lax.axis_index("slab")
    return slab // 2, slab % 2


def factor_kernel(halves, orders_ref, mine_ref, theirs_ref, out_ref, a_ref):
    _, core = position()
    order = orders_ref[lax.axis_index("blk")]
    for turn in range(2):
        @pl.when(core == turn)
        def _():
            for ref, half in ((mine_ref, halves[turn]), (theirs_ref, halves[1 - turn])):
                for t, (i, k) in enumerate(half):
                    i, k = i * LANES, k * LANES
                    a_ref[i : i + LANES, k : k + LANES] = assemble(ref[t], i, k, order)
    factor_all(a_ref)
    own_rows(a_ref, out_ref, lax.axis_index("slab") * out_ref.shape[0])


def factor_whole_kernel(s_ref, out_ref, a_ref):
    a_ref[...] = s_ref[...]
    factor_all(a_ref)
    own_rows(a_ref, out_ref, lax.axis_index("slab") * out_ref.shape[0])


def split_upper(total_ref, halves, core, mine_ref, give_ref):
    for turn in range(2):
        @pl.when(core == turn)
        def _():
            for ref, half in ((mine_ref, halves[turn]), (give_ref, halves[1 - turn])):
                for t, (i, k) in enumerate(half):
                    i, k = i * LANES, k * LANES
                    mirror = total_ref[k : k + LANES, i : i + LANES].T
                    ref[t] = total_ref[i : i + LANES, k : k + LANES] + mirror


def fetch(z_refs, use_x, slab, held_ref, sems, first):
    half = held_ref.shape[1]
    waits = []
    for t in range(2):
        rows = pl.ds(pl.multiple_of((slab * 2 + t) * half, half), half)
        copies = [
            pltpu.make_async_copy(z_ref.at[rows], held_ref.at[first + t], sems.at[first + t]) for z_ref in z_refs
        ]
        pl.when(use_x)(copies[0].start)
        pl.when(jnp.logical_not(use_x))(copies[1].start)
        waits.append(copies[0].wait)
    return waits


def near_kernel(
    halves, x_ref, y_ref, keep_ref, send_ref, cross_ref,
    side_mine_ref, side_give_ref, main_mine_ref, main_give_ref, main_ref, side_ref, held_ref, sems,
):
    chip, core = position()
    own, other = chip * 2 + core, chip * 2 + 1 - core
    half = held_ref.shape[1]
    waits = (
        fetch((x_ref, y_ref), chip == 0, own, held_ref, sems, 0)
        + fetch((x_ref, y_ref), chip == 1, own, held_ref, sems, 2)
        + fetch((x_ref, y_ref), chip == core, other, held_ref, sems, 4)
    )

    def add(t, sel_ref, left_ref, scale, total_ref, fresh):
        u = lax.dot_general(held_ref[t], sel_ref[...], NT, preferred_element_type=F32)
        left = left_ref[:, t % 2 * half : (t % 2 + 1) * half]
        part = jnp.dot(left, (u * scale).astype(BF16), preferred_element_type=F32)
        total_ref[...] = part if fresh else total_ref[...] + part

    for t, wait in enumerate(waits):
        wait()
        if t < 2:
            add(t, keep_ref, keep_ref, 0.5, main_ref, t == 0)
        elif t < 4:
            add(t, send_ref, send_ref, 0.5, side_ref, t == 2)
        else:
            pl.when(core == 0)(functools.partial(add, t, keep_ref, cross_ref, 1.0, main_ref, False))
            pl.when(core == 1)(functools.partial(add, t, send_ref, cross_ref, 1.0, side_ref, False))
    split_upper(side_ref, halves, core, side_mine_ref, side_give_ref)
    split_upper(main_ref, halves, core, main_mine_ref, main_give_ref)


def in_hbm(z):
    return pltpu.with_memory_space_constraint(z, pltpu.HBM)


def near(halves, x, y, keep, send, cross):
    size, depth = keep.shape
    blocks = (len(halves[0]), LANES, LANES)
    return pl.pallas_call(
        functools.partial(near_kernel, halves),
        out_shape=(jax.ShapeDtypeStruct(blocks, F32),) * 4,
        in_specs=[ANY, ANY, VMEM, VMEM, VMEM],
        out_specs=(VMEM,) * 4,
        scratch_shapes=[
            pltpu.VMEM((size, size), F32),
            pltpu.VMEM((size, size), F32),
            pltpu.VMEM((6, depth // 2, depth), BF16),
            pltpu.SemaphoreType.DMA((6,)),
        ],
        cost_estimate=pl.CostEstimate(
            flops=6 * depth * size * (depth + size), bytes_accessed=6 * depth * (depth + size), transcendentals=0
        ),
        name="near",
        compiler_params=pltpu.CompilerParams(vmem_limit_bytes=20 << 20),
    )(in_hbm(x), in_hbm(y), keep, send, cross)


def far_product_kernel(x_ref, y_ref, keep_ref, *refs):
    got_ref, (out_ref, held_ref, sems) = (refs[0] if len(refs) == 4 else None), refs[-3:]
    chip, core = position()
    half = held_ref.shape[1]
    holder = 1 - core if got_ref is None else core
    waits = fetch((x_ref, y_ref), chip == 0, (1 - chip) * 2 + holder, held_ref, sems, 0)
    for t, wait in enumerate(waits):
        wait()
        rows = slice(t * half, t * half + half)
        u = lax.dot_general(held_ref[t], keep_ref[...], NT, preferred_element_type=F32)
        if got_ref is not None:
            u = u + got_ref[rows, :].astype(F32)
        out_ref[rows, :] = u.astype(BF16)


def far_product(x, y, keep, *got):
    size, depth = keep.shape
    return pl.pallas_call(
        far_product_kernel,
        out_shape=jax.ShapeDtypeStruct((depth, size), BF16),
        in_specs=[ANY, ANY, VMEM] + [VMEM] * len(got),
        out_specs=VMEM,
        scratch_shapes=[pltpu.VMEM((2, depth // 2, depth), BF16), pltpu.SemaphoreType.DMA((2,))],
        cost_estimate=pl.CostEstimate(
            flops=2 * depth * depth * size, bytes_accessed=2 * depth * (depth + 2 * size), transcendentals=0
        ),
        name="far_product",
        compiler_params=pltpu.CompilerParams(vmem_limit_bytes=20 << 20),
    )(in_hbm(x), in_hbm(y), keep, *got)


def far_kernel(halves, sel_ref, both_ref, mine_ref, give_ref, total_ref):
    _, core = position()
    total_ref[...] = jnp.dot(sel_ref[...], both_ref[...], preferred_element_type=F32)
    split_upper(total_ref, halves, core, mine_ref, give_ref)


def select_columns(v, index):
    hot = (index[:, None] == lax.broadcasted_iota(jnp.int32, (index.shape[0], v.shape[1]), 1)).astype(BF16)
    return lax.dot_general(hot, v, NT, preferred_element_type=F32).astype(BF16)


def place(own, dest, groups):
    source = jnp.argmax(dest[None, :] == jnp.arange(groups, dtype=dest.dtype)[:, None], axis=1)
    pieces = own.reshape(groups, own.shape[0] // groups, own.shape[1])
    pieces = lax.all_to_all(pieces, "blk", 0, 0)
    pieces = jnp.take(pieces, source, axis=0)
    pieces = lax.all_to_all(pieces, "blk", 0, 0)
    return pieces.reshape(own.shape)


def two_chips(x, y, v, index, orders, dest):
    slabs, groups = lax.axis_size("slab"), lax.axis_size("blk")
    depth, size = v.shape[0], index.shape[1]
    halves = upper_blocks(size)
    half = len(halves[0])
    to_core = [(s, s ^ 1) for s in range(slabs)]
    to_chip = [(s, s ^ 2) for s in range(slabs)]
    blocks = jax.ShapeDtypeStruct((half, LANES, LANES), F32)
    chip, core = position()
    first, second = index

    send = lax.optimization_barrier(select_columns(v, jnp.where(chip == 0, second, first)))
    far = lax.ppermute(send, "slab", to_chip)
    keep = select_columns(v, jnp.where(chip == 0, first, second))
    cross = lax.ppermute(jnp.where(core == 0, send, keep), "slab", to_core)
    give = far_product(x, y, keep)
    got = lax.ppermute(give, "slab", to_core)
    side_mine, side_give, main_mine, main_give = near(halves, x, y, keep, send, cross)
    side_sum = side_mine + lax.ppermute(side_give, "slab", to_core)
    early = lax.ppermute(side_sum, "slab", to_chip)
    both = far_product(x, y, keep, got)
    main_sum = main_mine + lax.ppermute(main_give, "slab", to_core)
    far_mine, far_give = pl.pallas_call(
        functools.partial(far_kernel, halves),
        out_shape=(blocks, blocks),
        in_specs=[VMEM] * 2,
        out_specs=(VMEM, VMEM),
        scratch_shapes=[pltpu.VMEM((size, size), F32)],
        cost_estimate=pl.CostEstimate(
            flops=2 * depth * size * size, bytes_accessed=4 * depth * size, transcendentals=0
        ),
        name="far",
        compiler_params=pltpu.CompilerParams(vmem_limit_bytes=8 << 20),
    )(far, both)
    total = main_sum + early + (far_mine + lax.ppermute(far_give, "slab", to_core))
    schur = total * lax.ppermute(total, "slab", to_chip)
    other = lax.ppermute(schur, "slab", to_core)
    own = pl.pallas_call(
        functools.partial(factor_kernel, halves),
        out_shape=jax.ShapeDtypeStruct((size // slabs, size), F32),
        in_specs=[SMEM, VMEM, VMEM],
        out_specs=VMEM,
        scratch_shapes=[pltpu.VMEM((size, size), F32)],
        name="factor",
        compiler_params=pltpu.CompilerParams(vmem_limit_bytes=8 << 20),
    )(orders, schur, other)
    return place(own, dest, groups)


def any_chips(x, y, v, index, orders, dest):
    slabs, groups = lax.axis_size("slab"), lax.axis_size("blk")
    first, second = index
    order = orders[lax.axis_index("blk")]
    size = first.shape[0]
    share = size // slabs
    slab = lax.axis_index("slab")
    row_start = slab * share

    def pairing(z, index):
        picked = select_columns(v, index)
        every = lax.all_gather(picked, "slab", axis=1, tiled=True)
        c = jnp.dot(every, z, preferred_element_type=F32).astype(BF16)
        return lax.dot_general(c, picked, NT, preferred_element_type=F32)

    both = jnp.concatenate([pairing(x, first), pairing(y, second)], axis=1)
    both = lax.psum_scatter(both, "slab", scatter_dimension=0, tiled=True)
    schur = both[:, :size] * both[:, size:]
    row_ids = row_start + jnp.arange(share, dtype=jnp.int32)
    col_ids = jnp.arange(size, dtype=jnp.int32)
    mask = (row_ids[:, None] < order) & (col_ids[None, :] < order)
    schur = jnp.where(mask, schur, 0.0) + (row_ids[:, None] == col_ids[None, :]).astype(F32)
    whole = lax.all_gather(schur, "slab", axis=0, tiled=True)
    whole = 0.5 * (whole + whole.T)
    own = pl.pallas_call(
        factor_whole_kernel,
        out_shape=jax.ShapeDtypeStruct((share, size), F32),
        in_specs=[VMEM],
        out_specs=VMEM,
        scratch_shapes=[pltpu.VMEM((size, size), F32)],
        name="factor",
        compiler_params=pltpu.CompilerParams(vmem_limit_bytes=8 << 20),
    )(whole)
    return place(own, dest, groups)


def on_device(xinv, ymat, basis, pair_index, orders, dest):
    body = two_chips if lax.axis_size("slab") == 4 else any_chips
    return body(xinv[0], ymat[0], basis[0], pair_index[0], orders, dest)[None]


def solution(mesh):
    return jax.shard_map(
        on_device,
        mesh=mesh,
        in_specs=(
            P("blk", None, "slab"),
            P("blk", None, "slab"),
            P("blk", "slab", None),
            P("blk", None, None),
            P(),
            P(),
        ),
        out_specs=P("blk", "slab", None),
        check_vma=False,
    )
```

```python
import functools

import jax
import jax.numpy as jnp
from jax import lax
from jax.experimental import pallas as pl
from jax.experimental.pallas import tpu as pltpu
from jax.sharding import PartitionSpec as P


F32 = jnp.float32
BF16 = jnp.bfloat16
LANES = 128
MICRO = 8
GROUP = 4
AHEAD = 1
VMEM = pl.BlockSpec(memory_space=pltpu.VMEM)
SMEM = pl.BlockSpec(memory_space=pltpu.SMEM)
ANY = pl.BlockSpec(memory_space=pl.ANY)
TN = (((0,), (0,)), ((), ()))
NT = (((1,), (1,)), ((), ()))


def dot_f32(a, b, dims):
    dot = functools.partial(lax.dot_general, dimension_numbers=dims, preferred_element_type=F32)
    a_hi, b_hi = a.astype(BF16), b.astype(BF16)
    a_lo = (a - a_hi.astype(F32)).astype(BF16)
    b_lo = (b - b_hi.astype(F32)).astype(BF16)
    return dot(a_hi, b_hi) + (dot(a_hi, b_lo) + dot(a_lo, b_hi))


def lane_splat(x, lane):
    return jnp.take_along_axis(x, jnp.full((MICRO, LANES), lane, jnp.int32), axis=1)


def row_splat(x, row):
    return jnp.broadcast_to(x[row : row + 1, :], (MICRO, x.shape[1]))


def by_tile(f, *wide):
    tiles = [f(*[x[:, t : t + LANES] for x in wide]) for t in range(0, wide[0].shape[1], LANES)]
    return tiles[0] if len(tiles) == 1 else jnp.concatenate(tiles, axis=1)


def factor_rows(a_ref, start, width):
    cols = None
    span = slice(start, start + width)
    count = LANES // MICRO
    for m in range(count):
        base = MICRO * m
        here = slice(start + base, start + base + MICRO)
        rows = a_ref[here, span]
        if cols is None:
            cols = [lane_splat(rows[:, :LANES], base + k) for k in range(MICRO)]
        low = {(i, k): row_splat(cols[k], i) for k in range(MICRO) for i in range(k, MICRO)}
        inv = []
        for k in range(MICRO):
            inv.append(lax.rsqrt(low[k, k]))
            for i in range(k + 1, MICRO):
                low[i, k] = low[i, k] * inv[k]
            for j in range(k + 1, MICRO):
                for i in range(j, MICRO):
                    low[i, j] = low[i, j] - low[i, k] * low[j, k]
        wide = [row_splat(rows, i) for i in range(MICRO)]
        for k in range(MICRO):
            wide[k] = by_tile(lambda x: x * inv[k], wide[k])
            for i in range(k + 1, MICRO):
                wide[i] = by_tile(lambda x, u: x - low[i, k] * u, wide[i], wide[k])
        sub = lax.broadcasted_iota(jnp.int32, (MICRO, width), 0)
        lane = lax.broadcasted_iota(jnp.int32, (MICRO, width), 1)
        packed = wide[0]
        for k in range(1, MICRO):
            packed = jnp.where(sub == k, wide[k], packed)
        a_ref[here, span] = jnp.where(lane >= sub + base, packed, 0.0)
        group_end = (m // GROUP + 1) * GROUP
        cols = None
        for later in range(m + 1, min(group_end + AHEAD, count)):
            there = slice(start + MICRO * later, start + MICRO * later + MICRO)
            rest = a_ref[there, span]
            head = rest[:, :LANES]
            part = [lane_splat(head, base + k) for k in range(MICRO)]
            for k in range(MICRO):
                for j in range(k):
                    part[k] = part[k] - low[k, j] * part[j]
                part[k] = part[k] * inv[k]
            if later == m + 1:
                cols = [lane_splat(head, MICRO * later + j) for j in range(MICRO)]
                for k in range(MICRO):
                    for j in range(MICRO):
                        cols[j] = cols[j] - part[k] * row_splat(part[k], j)
            for k in range(MICRO):
                rest = by_tile(lambda x, u: x - part[k] * u, rest, wide[k])
            a_ref[there, span] = rest
        if m + 1 == group_end and group_end + AHEAD < count:
            done = a_ref[start + MICRO * (group_end - GROUP) : start + MICRO * group_end, span]
            first = MICRO * (group_end + AHEAD)
            there = slice(start + first, start + LANES)
            a_ref[there, span] = a_ref[there, span] - dot_f32(done[:, :LANES], done, TN)[first:]


def factor_all(a_ref, done=0):
    size = a_ref.shape[0]
    for start in range(0, size, LANES):
        if start >= done:
            factor_rows(a_ref, start, size - start)
        for row in range(start + LANES, size, LANES):
            left = a_ref[start : start + LANES, row : row + LANES]
            right = a_ref[start : start + LANES, row:]
            a_ref[row : row + LANES, row:] = a_ref[row : row + LANES, row:] - dot_f32(left, right, TN)


def own_rows(a_ref, out_ref, row_start):
    share, size = out_ref.shape
    base = pl.multiple_of(row_start // LANES * LANES, LANES)
    inner = row_start - base
    for q in range(0, size, LANES):
        block = a_ref[q : q + LANES, pl.ds(base, LANES)]
        block = jnp.where(q <= base, block, 0.0).T
        if share % LANES:
            keep = (
                lax.broadcasted_iota(jnp.int32, (share, LANES), 0) + inner
                == lax.broadcasted_iota(jnp.int32, (share, LANES), 1)
            ).astype(F32)
            block = lax.dot_general(
                keep, block, (((1,), (0,)), ((), ())),
                precision=lax.Precision.HIGHEST, preferred_element_type=F32,
            )
        out_ref[:, q : q + LANES] = block


def assemble(block, row, col, order):
    rows = lax.broadcasted_iota(jnp.int32, block.shape, 0) + row
    cols = lax.broadcasted_iota(jnp.int32, block.shape, 1) + col
    return jnp.where((rows < order) & (cols < order), block, 0.0) + (rows == cols).astype(F32)


def deal(size):
    count = size // LANES
    items = [(i, k) for i in range(count) for k in range(i, count) if i < k or i % 2 == 0]
    first = [item for item in items if item[0] == 0]
    rest = [item for item in items if item[0] > 0]
    middle, centre = len(first) // 2, len(rest) // 2
    return (first[:middle], rest[:centre]), (first[middle:], rest[centre:])


def triangle():
    row = lax.broadcasted_iota(jnp.int32, (LANES, LANES), 0)
    return row - lax.broadcasted_iota(jnp.int32, (LANES, LANES), 1)


def packed_shape(hands):
    return (len(hands[0][0]) + len(hands[0][1])) * LANES + MICRO, LANES


def deal_out(total_ref, hands, core, mine_ref, give_ref):
    def sym(i, k):
        i, k = i * LANES, k * LANES
        return total_ref[i : i + LANES, k : k + LANES] + total_ref[k : k + LANES, i : i + LANES].T

    for turn in range(2):
        @pl.when(core == turn)
        def _():
            for ref, hand in ((mine_ref, hands[turn]), (give_ref, hands[1 - turn])):
                items = hand[0] + hand[1]
                tail = len(items) * LANES
                ref[tail:, :] = jnp.zeros((ref.shape[0] - tail, LANES), F32)
                for t, (i, k) in enumerate(items):
                    block = sym(i, k)
                    if i == k:
                        other = sym(i + 1, i + 1)
                        diagonal = jnp.sum(jnp.where(triangle() == 0, other, 0.0), axis=0, keepdims=True)
                        ref[tail + i // 2 : tail + i // 2 + 1, :] = diagonal
                        block = jnp.where(triangle() >= 0, block, other)
                    ref[t * LANES : t * LANES + LANES, :] = block


def position():
    slab = lax.axis_index("slab")
    return slab // 2, slab % 2


def place_blocks(a_ref, order, items, block_of, row_of, wanted):
    for t, (i, k) in enumerate(items):
        block = block_of(t)
        parts = [((i, k), block)]
        if i == k:
            flipped = block.T
            one = jnp.where(triangle() >= 0, block, flipped)
            parts = [((i, i), one)]
            if wanted(i + 1):
                other = jnp.where(triangle() < 0, block, flipped)
                other = jnp.where(triangle() == 0, row_of(i // 2), other)
                parts.append(((i + 1, i + 1), other))
        for (i, k), block in parts:
            if wanted(i):
                i, k = i * LANES, k * LANES
                a_ref[i : i + LANES, k : k + LANES] = assemble(block, i, k, order)


def factor_first_kernel(hands, orders_ref, mine_ref, theirs_ref, a_ref):
    _, core = position()
    order = orders_ref[lax.axis_index("blk")]
    for turn in range(2):
        @pl.when(core == turn)
        def _():
            for ref, hand in ((mine_ref, hands[turn]), (theirs_ref, hands[1 - turn])):
                block_of = lambda t: ref[t * LANES : t * LANES + LANES, :]
                place_blocks(a_ref, order, hand[0], block_of, None, lambda i: i == 0)
    factor_rows(a_ref, 0, a_ref.shape[1])


def factor_rest_kernel(
    hands, orders_ref, top_ref, mine_ref, theirs_ref, mine_rest_ref, theirs_rest_ref, out_ref, a_ref
):
    _, core = position()
    order = orders_ref[lax.axis_index("blk")]
    done = top_ref.shape[0]
    a_ref[:done, :] = top_ref[...]
    for turn in range(2):
        @pl.when(core == turn)
        def _():
            for ref, rest_ref, hand in (
                (mine_ref, mine_rest_ref, hands[turn]),
                (theirs_ref, theirs_rest_ref, hands[1 - turn]),
            ):
                tail = len(hand[1]) * LANES
                row_of = lambda e: rest_ref[tail + e : tail + e + 1, :]
                for part, part_ref in ((hand[0], ref), (hand[1], rest_ref)):
                    block_of = lambda t: part_ref[t * LANES : t * LANES + LANES, :]
                    place_blocks(a_ref, order, part, block_of, row_of, lambda i: i > 0)
    factor_all(a_ref, done)
    own_rows(a_ref, out_ref, lax.axis_index("slab") * out_ref.shape[0])


def factor_whole_kernel(s_ref, out_ref, a_ref):
    a_ref[...] = s_ref[...]
    factor_all(a_ref)
    own_rows(a_ref, out_ref, lax.axis_index("slab") * out_ref.shape[0])


def fetch(z_refs, use_x, slab, held_ref, sems, first):
    half = held_ref.shape[1]
    waits = []
    for t in range(2):
        rows = pl.ds(pl.multiple_of((slab * 2 + t) * half, half), half)
        copies = [
            pltpu.make_async_copy(z_ref.at[rows], held_ref.at[first + t], sems.at[first + t]) for z_ref in z_refs
        ]
        pl.when(use_x)(copies[0].start)
        pl.when(jnp.logical_not(use_x))(copies[1].start)
        waits.append(copies[0].wait)
    return waits


def near_kernel(
    hands, x_ref, y_ref, keep_ref, send_ref, cross_ref,
    side_mine_ref, side_give_ref, main_mine_ref, main_give_ref, main_ref, side_ref, held_ref, sems,
):
    chip, core = position()
    own, other = chip * 2 + core, chip * 2 + 1 - core
    half = held_ref.shape[1]
    waits = (
        fetch((x_ref, y_ref), chip == 0, own, held_ref, sems, 0)
        + fetch((x_ref, y_ref), chip == 1, own, held_ref, sems, 2)
        + fetch((x_ref, y_ref), chip == core, other, held_ref, sems, 4)
    )

    def add(t, sel_ref, left_ref, scale, total_ref, fresh):
        u = lax.dot_general(held_ref[t], sel_ref[...], NT, preferred_element_type=F32)
        left = left_ref[:, t % 2 * half : (t % 2 + 1) * half]
        part = jnp.dot(left, (u * scale).astype(BF16), preferred_element_type=F32)
        total_ref[...] = part if fresh else total_ref[...] + part

    for t, wait in enumerate(waits):
        wait()
        if t < 2:
            add(t, keep_ref, keep_ref, 0.5, main_ref, t == 0)
        elif t < 4:
            add(t, send_ref, send_ref, 0.5, side_ref, t == 2)
        else:
            pl.when(core == 0)(functools.partial(add, t, keep_ref, cross_ref, 1.0, main_ref, False))
            pl.when(core == 1)(functools.partial(add, t, send_ref, cross_ref, 1.0, side_ref, False))
    deal_out(side_ref, hands, core, side_mine_ref, side_give_ref)
    deal_out(main_ref, hands, core, main_mine_ref, main_give_ref)


def in_hbm(z):
    return pltpu.with_memory_space_constraint(z, pltpu.HBM)


def near(hands, x, y, keep, send, cross):
    size, depth = keep.shape
    blocks = packed_shape(hands)
    return pl.pallas_call(
        functools.partial(near_kernel, hands),
        out_shape=(jax.ShapeDtypeStruct(blocks, F32),) * 4,
        in_specs=[ANY, ANY, VMEM, VMEM, VMEM],
        out_specs=(VMEM,) * 4,
        scratch_shapes=[
            pltpu.VMEM((size, size), F32),
            pltpu.VMEM((size, size), F32),
            pltpu.VMEM((6, depth // 2, depth), BF16),
            pltpu.SemaphoreType.DMA((6,)),
        ],
        cost_estimate=pl.CostEstimate(
            flops=6 * depth * size * (depth + size), bytes_accessed=6 * depth * (depth + size), transcendentals=0
        ),
        name="near",
        compiler_params=pltpu.CompilerParams(vmem_limit_bytes=20 << 20),
    )(in_hbm(x), in_hbm(y), keep, send, cross)


def far_product_kernel(x_ref, y_ref, keep_ref, *refs):
    got_ref, (out_ref, held_ref, sems) = (refs[0] if len(refs) == 4 else None), refs[-3:]
    chip, core = position()
    half = held_ref.shape[1]
    holder = 1 - core if got_ref is None else core
    waits = fetch((x_ref, y_ref), chip == 0, (1 - chip) * 2 + holder, held_ref, sems, 0)
    for t, wait in enumerate(waits):
        wait()
        rows = slice(t * half, t * half + half)
        u = lax.dot_general(held_ref[t], keep_ref[...], NT, preferred_element_type=F32)
        if got_ref is not None:
            u = u + got_ref[rows, :].astype(F32)
        out_ref[rows, :] = u.astype(BF16)


def far_product(x, y, keep, *got):
    size, depth = keep.shape
    return pl.pallas_call(
        far_product_kernel,
        out_shape=jax.ShapeDtypeStruct((depth, size), BF16),
        in_specs=[ANY, ANY, VMEM] + [VMEM] * len(got),
        out_specs=VMEM,
        scratch_shapes=[pltpu.VMEM((2, depth // 2, depth), BF16), pltpu.SemaphoreType.DMA((2,))],
        cost_estimate=pl.CostEstimate(
            flops=2 * depth * depth * size, bytes_accessed=2 * depth * (depth + 2 * size), transcendentals=0
        ),
        name="far_product",
        compiler_params=pltpu.CompilerParams(vmem_limit_bytes=20 << 20),
    )(in_hbm(x), in_hbm(y), keep, *got)


def far_kernel(hands, sel_ref, both_ref, mine_ref, give_ref, total_ref):
    _, core = position()
    total_ref[...] = jnp.dot(sel_ref[...], both_ref[...], preferred_element_type=F32)
    deal_out(total_ref, hands, core, mine_ref, give_ref)


def select_columns(v, index):
    hot = (index[:, None] == lax.broadcasted_iota(jnp.int32, (index.shape[0], v.shape[1]), 1)).astype(BF16)
    return lax.dot_general(hot, v, NT, preferred_element_type=F32).astype(BF16)


def place(own, dest, groups):
    source = jnp.argmax(dest[None, :] == jnp.arange(groups, dtype=dest.dtype)[:, None], axis=1)
    pieces = own.reshape(groups, own.shape[0] // groups, own.shape[1])
    pieces = lax.all_to_all(pieces, "blk", 0, 0)
    pieces = jnp.take(pieces, source, axis=0)
    pieces = lax.all_to_all(pieces, "blk", 0, 0)
    return pieces.reshape(own.shape)


def two_chips(x, y, v, index, orders, dest):
    slabs, groups = lax.axis_size("slab"), lax.axis_size("blk")
    depth, size = v.shape[0], index.shape[1]
    hands = deal(size)
    top = len(hands[0][0]) * LANES
    to_core = [(s, s ^ 1) for s in range(slabs)]
    to_chip = [(s, s ^ 2) for s in range(slabs)]
    blocks = jax.ShapeDtypeStruct(packed_shape(hands), F32)
    chip, core = position()
    first, second = index

    send = lax.optimization_barrier(select_columns(v, jnp.where(chip == 0, second, first)))
    far = lax.ppermute(send, "slab", to_chip)
    keep = select_columns(v, jnp.where(chip == 0, first, second))
    cross = lax.ppermute(jnp.where(core == 0, send, keep), "slab", to_core)
    give = far_product(x, y, keep)
    got = lax.ppermute(give, "slab", to_core)
    side_mine, side_give, main_mine, main_give = near(hands, x, y, keep, send, cross)
    side_sum = side_mine + lax.ppermute(side_give, "slab", to_core)
    early = lax.ppermute(side_sum, "slab", to_chip)
    both = far_product(x, y, keep, got)
    main_sum = main_mine + lax.ppermute(main_give, "slab", to_core)
    far_mine, far_give = pl.pallas_call(
        functools.partial(far_kernel, hands),
        out_shape=(blocks, blocks),
        in_specs=[VMEM] * 2,
        out_specs=(VMEM, VMEM),
        scratch_shapes=[pltpu.VMEM((size, size), F32)],
        cost_estimate=pl.CostEstimate(
            flops=2 * depth * size * size, bytes_accessed=4 * depth * size, transcendentals=0
        ),
        name="far",
        compiler_params=pltpu.CompilerParams(vmem_limit_bytes=8 << 20),
    )(far, both)
    total = main_sum + early + (far_mine + lax.ppermute(far_give, "slab", to_core))
    first_got = lax.ppermute(total[:top], "slab", to_chip)
    rest_got = lax.ppermute(total[top:], "slab", to_chip)
    schur = total[:top] * first_got
    other = lax.ppermute(schur, "slab", to_core)
    upper = pl.pallas_call(
        functools.partial(factor_first_kernel, hands),
        out_shape=jax.ShapeDtypeStruct((LANES, size), F32),
        in_specs=[SMEM, VMEM, VMEM],
        out_specs=VMEM,
        cost_estimate=pl.CostEstimate(
            flops=LANES * LANES * size, bytes_accessed=16 * LANES * size, transcendentals=LANES
        ),
        name="factor_first",
        compiler_params=pltpu.CompilerParams(vmem_limit_bytes=8 << 20),
    )(orders, schur, other)
    schur_rest = total[top:] * rest_got
    other_rest = lax.ppermute(schur_rest, "slab", to_core)
    own = pl.pallas_call(
        functools.partial(factor_rest_kernel, hands),
        out_shape=jax.ShapeDtypeStruct((size // slabs, size), F32),
        in_specs=[SMEM] + [VMEM] * 5,
        out_specs=VMEM,
        scratch_shapes=[pltpu.VMEM((size, size), F32)],
        name="factor_rest",
        compiler_params=pltpu.CompilerParams(vmem_limit_bytes=8 << 20),
    )(orders, upper, schur, other, schur_rest, other_rest)
    return place(own, dest, groups)


def any_chips(x, y, v, index, orders, dest):
    slabs, groups = lax.axis_size("slab"), lax.axis_size("blk")
    first, second = index
    order = orders[lax.axis_index("blk")]
    size = first.shape[0]
    share = size // slabs
    slab = lax.axis_index("slab")
    row_start = slab * share

    def pairing(z, index):
        picked = select_columns(v, index)
        every = lax.all_gather(picked, "slab", axis=1, tiled=True)
        c = jnp.dot(every, z, preferred_element_type=F32).astype(BF16)
        return lax.dot_general(c, picked, NT, preferred_element_type=F32)

    both = jnp.concatenate([pairing(x, first), pairing(y, second)], axis=1)
    both = lax.psum_scatter(both, "slab", scatter_dimension=0, tiled=True)
    schur = both[:, :size] * both[:, size:]
    row_ids = row_start + jnp.arange(share, dtype=jnp.int32)
    col_ids = jnp.arange(size, dtype=jnp.int32)
    mask = (row_ids[:, None] < order) & (col_ids[None, :] < order)
    schur = jnp.where(mask, schur, 0.0) + (row_ids[:, None] == col_ids[None, :]).astype(F32)
    whole = lax.all_gather(schur, "slab", axis=0, tiled=True)
    whole = 0.5 * (whole + whole.T)
    own = pl.pallas_call(
        factor_whole_kernel,
        out_shape=jax.ShapeDtypeStruct((share, size), F32),
        in_specs=[VMEM],
        out_specs=VMEM,
        scratch_shapes=[pltpu.VMEM((size, size), F32)],
        name="factor",
        compiler_params=pltpu.CompilerParams(vmem_limit_bytes=8 << 20),
    )(whole)
    return place(own, dest, groups)


def on_device(xinv, ymat, basis, pair_index, orders, dest):
    body = two_chips if lax.axis_size("slab") == 4 else any_chips
    return body(xinv[0], ymat[0], basis[0], pair_index[0], orders, dest)[None]


def solution(mesh):
    return jax.shard_map(
        on_device,
        mesh=mesh,
        in_specs=(
            P("blk", None, "slab"),
            P("blk", None, "slab"),
            P("blk", "slab", None),
            P("blk", None, None),
            P(),
            P(),
        ),
        out_specs=P("blk", "slab", None),
        check_vma=False,
    )
```

```python
import functools

import jax
import jax.numpy as jnp
from jax import lax
from jax.experimental import pallas as pl
from jax.experimental.pallas import tpu as pltpu
from jax.sharding import PartitionSpec as P


F32 = jnp.float32
BF16 = jnp.bfloat16
LANES = 128
MICRO = 8
GROUP = 8
VMEM = pl.BlockSpec(memory_space=pltpu.VMEM)
SMEM = pl.BlockSpec(memory_space=pltpu.SMEM)
ANY = pl.BlockSpec(memory_space=pl.ANY)
TN = (((0,), (0,)), ((), ()))
NT = (((1,), (1,)), ((), ()))


def dot_f32(a, b, dims):
    dot = functools.partial(lax.dot_general, dimension_numbers=dims, preferred_element_type=F32)
    a_hi, b_hi = a.astype(BF16), b.astype(BF16)
    a_lo = (a - a_hi.astype(F32)).astype(BF16)
    b_lo = (b - b_hi.astype(F32)).astype(BF16)
    return dot(a_hi, b_hi) + (dot(a_hi, b_lo) + dot(a_lo, b_hi))


def lane_splat(x, lane):
    return jnp.take_along_axis(x, jnp.full((MICRO, LANES), lane, jnp.int32), axis=1)


def row_splat(x, row):
    return jnp.broadcast_to(x[row : row + 1, :], (MICRO, x.shape[1]))


def by_tile(f, *wide):
    tiles = [f(*[x[:, t : t + LANES] for x in wide]) for t in range(0, wide[0].shape[1], LANES)]
    return tiles[0] if len(tiles) == 1 else jnp.concatenate(tiles, axis=1)


def factor_rows(a_ref, start, width):
    cols = None
    span = slice(start, start + width)
    count = LANES // MICRO
    for m in range(count):
        base = MICRO * m
        here = slice(start + base, start + base + MICRO)
        rows = a_ref[here, span]
        if cols is None:
            cols = [lane_splat(rows[:, :LANES], base + k) for k in range(MICRO)]
        low = {(i, k): row_splat(cols[k], i) for k in range(MICRO) for i in range(k, MICRO)}
        inv = []
        for k in range(MICRO):
            inv.append(lax.rsqrt(low[k, k]))
            for i in range(k + 1, MICRO):
                low[i, k] = low[i, k] * inv[k]
            for j in range(k + 1, MICRO):
                for i in range(j, MICRO):
                    low[i, j] = low[i, j] - low[i, k] * low[j, k]
        sub = lax.broadcasted_iota(jnp.int32, (MICRO, LANES), 0)
        wide = []
        left = rows
        for k in range(MICRO):
            u = by_tile(lambda x: x * inv[k], row_splat(left, k))
            wide.append(u)
            if k + 1 < MICRO:
                column = jnp.where(sub == k + 1, low[k + 1, k], 0.0)
                for i in range(k + 2, MICRO):
                    column = jnp.where(sub == i, low[i, k], column)
                left = by_tile(lambda x, y: x - column * y, left, u)
        scale = inv[0]
        for k in range(1, MICRO):
            scale = jnp.where(sub == k, inv[k], scale)
        upper = lax.broadcasted_iota(jnp.int32, (MICRO, LANES), 1) >= sub + base
        a_ref[here, start : start + LANES] = jnp.where(upper, left[:, :LANES] * scale, 0.0)
        for t in range(LANES, width, LANES):
            a_ref[here, start + t : start + t + LANES] = left[:, t : t + LANES] * scale
        group_end = (m // GROUP + 1) * GROUP
        cols = None
        for later in range(m + 1, min(group_end + 1, count)):
            there = slice(start + MICRO * later, start + MICRO * later + MICRO)
            rest = a_ref[there, span]
            head = rest[:, :LANES]
            part = [lane_splat(head, base + k) for k in range(MICRO)]
            for k in range(MICRO):
                for j in range(k):
                    part[k] = part[k] - low[k, j] * part[j]
                part[k] = part[k] * inv[k]
            if later == m + 1:
                cols = [lane_splat(head, MICRO * later + j) for j in range(MICRO)]
                for k in range(MICRO):
                    for j in range(MICRO):
                        cols[j] = cols[j] - part[k] * row_splat(part[k], j)
            for k in range(MICRO):
                rest = by_tile(lambda x, u: x - part[k] * u, rest, wide[k])
            a_ref[there, span] = rest
        if m + 1 == group_end and group_end + 1 < count:
            done = a_ref[start + MICRO * (group_end - GROUP) : start + MICRO * group_end, span]
            first = MICRO * (group_end + 1)
            there = slice(start + first, start + LANES)
            a_ref[there, span] = a_ref[there, span] - dot_f32(done[:, :LANES], done, TN)[first:]


def factor_all(a_ref, done=0):
    size = a_ref.shape[0]
    for start in range(0, size, LANES):
        if start >= done:
            factor_rows(a_ref, start, size - start)
        for row in range(start + LANES, size, LANES):
            left = a_ref[start : start + LANES, row : row + LANES]
            right = a_ref[start : start + LANES, row:]
            a_ref[row : row + LANES, row:] = a_ref[row : row + LANES, row:] - dot_f32(left, right, TN)


def own_rows(a_ref, out_ref, row_start):
    share, size = out_ref.shape
    base = pl.multiple_of(row_start // LANES * LANES, LANES)
    inner = row_start - base
    for q in range(0, size, LANES):
        block = a_ref[q : q + LANES, pl.ds(base, LANES)]
        block = jnp.where(q <= base, block, 0.0).T
        if share % LANES:
            keep = (
                lax.broadcasted_iota(jnp.int32, (share, LANES), 0) + inner
                == lax.broadcasted_iota(jnp.int32, (share, LANES), 1)
            ).astype(F32)
            block = lax.dot_general(
                keep, block, (((1,), (0,)), ((), ())),
                precision=lax.Precision.HIGHEST, preferred_element_type=F32,
            )
        out_ref[:, q : q + LANES] = block


def assemble(block, row, col, order):
    rows = lax.broadcasted_iota(jnp.int32, block.shape, 0) + row
    cols = lax.broadcasted_iota(jnp.int32, block.shape, 1) + col
    return jnp.where((rows < order) & (cols < order), block, 0.0) + (rows == cols).astype(F32)


def deal(size):
    count = size // LANES
    items = [(i, k) for i in range(count) for k in range(i, count) if i < k or i % 2 == 0]
    first = [item for item in items if item[0] == 0]
    rest = [item for item in items if item[0] > 0]
    middle, centre = len(first) // 2, len(rest) // 2
    return (first[:middle], rest[:centre]), (first[middle:], rest[centre:])


def triangle():
    row = lax.broadcasted_iota(jnp.int32, (LANES, LANES), 0)
    return row - lax.broadcasted_iota(jnp.int32, (LANES, LANES), 1)


def packed_shape(hands):
    return (len(hands[0][0]) + len(hands[0][1])) * LANES + MICRO, LANES


def deal_out(total_ref, hands, core, mine_ref, give_ref):
    def sym(i, k):
        i, k = i * LANES, k * LANES
        return total_ref[i : i + LANES, k : k + LANES] + total_ref[k : k + LANES, i : i + LANES].T

    for turn in range(2):
        @pl.when(core == turn)
        def _():
            for ref, hand in ((mine_ref, hands[turn]), (give_ref, hands[1 - turn])):
                items = hand[0] + hand[1]
                tail = len(items) * LANES
                ref[tail:, :] = jnp.zeros((ref.shape[0] - tail, LANES), F32)
                for t, (i, k) in enumerate(items):
                    block = sym(i, k)
                    if i == k:
                        other = sym(i + 1, i + 1)
                        diagonal = jnp.sum(jnp.where(triangle() == 0, other, 0.0), axis=0, keepdims=True)
                        ref[tail + i // 2 : tail + i // 2 + 1, :] = diagonal
                        block = jnp.where(triangle() >= 0, block, other)
                    ref[t * LANES : t * LANES + LANES, :] = block


def position():
    slab = lax.axis_index("slab")
    return slab // 2, slab % 2


def place_blocks(a_ref, order, items, block_of, row_of, wanted):
    for t, (i, k) in enumerate(items):
        block = block_of(t)
        parts = [((i, k), block)]
        if i == k:
            flipped = block.T
            one = jnp.where(triangle() >= 0, block, flipped)
            parts = [((i, i), one)]
            if wanted(i + 1):
                other = jnp.where(triangle() < 0, block, flipped)
                other = jnp.where(triangle() == 0, row_of(i // 2), other)
                parts.append(((i + 1, i + 1), other))
        for (i, k), block in parts:
            if wanted(i):
                i, k = i * LANES, k * LANES
                a_ref[i : i + LANES, k : k + LANES] = assemble(block, i, k, order)


def factor_first_kernel(hands, orders_ref, mine_ref, theirs_ref, a_ref):
    _, core = position()
    order = orders_ref[lax.axis_index("blk")]
    for turn in range(2):
        @pl.when(core == turn)
        def _():
            for ref, hand in ((mine_ref, hands[turn]), (theirs_ref, hands[1 - turn])):
                block_of = lambda t: ref[t * LANES : t * LANES + LANES, :]
                place_blocks(a_ref, order, hand[0], block_of, None, lambda i: i == 0)
    factor_rows(a_ref, 0, a_ref.shape[1])


def factor_rest_kernel(
    hands, orders_ref, top_ref, mine_ref, theirs_ref, mine_rest_ref, theirs_rest_ref, out_ref, a_ref
):
    _, core = position()
    order = orders_ref[lax.axis_index("blk")]
    done = top_ref.shape[0]
    a_ref[:done, :] = top_ref[...]
    for turn in range(2):
        @pl.when(core == turn)
        def _():
            for ref, rest_ref, hand in (
                (mine_ref, mine_rest_ref, hands[turn]),
                (theirs_ref, theirs_rest_ref, hands[1 - turn]),
            ):
                tail = len(hand[1]) * LANES
                row_of = lambda e: rest_ref[tail + e : tail + e + 1, :]
                for part, part_ref in ((hand[0], ref), (hand[1], rest_ref)):
                    block_of = lambda t: part_ref[t * LANES : t * LANES + LANES, :]
                    place_blocks(a_ref, order, part, block_of, row_of, lambda i: i > 0)
    factor_all(a_ref, done)
    own_rows(a_ref, out_ref, lax.axis_index("slab") * out_ref.shape[0])


def factor_whole_kernel(s_ref, out_ref, a_ref):
    a_ref[...] = s_ref[...]
    factor_all(a_ref)
    own_rows(a_ref, out_ref, lax.axis_index("slab") * out_ref.shape[0])


def fetch(z_refs, use_x, slab, held_ref, sems, first):
    half = held_ref.shape[1]
    waits = []
    for t in range(2):
        rows = pl.ds(pl.multiple_of((slab * 2 + t) * half, half), half)
        copies = [
            pltpu.make_async_copy(z_ref.at[rows], held_ref.at[first + t], sems.at[first + t]) for z_ref in z_refs
        ]
        pl.when(use_x)(copies[0].start)
        pl.when(jnp.logical_not(use_x))(copies[1].start)
        waits.append(copies[0].wait)
    return waits


def near_kernel(
    hands, x_ref, y_ref, keep_ref, send_ref, cross_ref,
    side_mine_ref, side_give_ref, main_mine_ref, main_give_ref, main_ref, side_ref, held_ref, sems,
):
    chip, core = position()
    own, other = chip * 2 + core, chip * 2 + 1 - core
    half = held_ref.shape[1]
    waits = (
        fetch((x_ref, y_ref), chip == 0, own, held_ref, sems, 0)
        + fetch((x_ref, y_ref), chip == 1, own, held_ref, sems, 2)
        + fetch((x_ref, y_ref), chip == core, other, held_ref, sems, 4)
    )

    def add(t, sel_ref, left_ref, scale, total_ref, fresh):
        u = lax.dot_general(held_ref[t], sel_ref[...], NT, preferred_element_type=F32)
        left = left_ref[:, t % 2 * half : (t % 2 + 1) * half]
        part = jnp.dot(left, (u * scale).astype(BF16), preferred_element_type=F32)
        total_ref[...] = part if fresh else total_ref[...] + part

    for t, wait in enumerate(waits):
        wait()
        if t < 2:
            add(t, keep_ref, keep_ref, 0.5, main_ref, t == 0)
        elif t < 4:
            add(t, send_ref, send_ref, 0.5, side_ref, t == 2)
        else:
            pl.when(core == 0)(functools.partial(add, t, keep_ref, cross_ref, 1.0, main_ref, False))
            pl.when(core == 1)(functools.partial(add, t, send_ref, cross_ref, 1.0, side_ref, False))
    deal_out(side_ref, hands, core, side_mine_ref, side_give_ref)
    deal_out(main_ref, hands, core, main_mine_ref, main_give_ref)


def in_hbm(z):
    return pltpu.with_memory_space_constraint(z, pltpu.HBM)


def near(hands, x, y, keep, send, cross):
    size, depth = keep.shape
    blocks = packed_shape(hands)
    return pl.pallas_call(
        functools.partial(near_kernel, hands),
        out_shape=(jax.ShapeDtypeStruct(blocks, F32),) * 4,
        in_specs=[ANY, ANY, VMEM, VMEM, VMEM],
        out_specs=(VMEM,) * 4,
        scratch_shapes=[
            pltpu.VMEM((size, size), F32),
            pltpu.VMEM((size, size), F32),
            pltpu.VMEM((6, depth // 2, depth), BF16),
            pltpu.SemaphoreType.DMA((6,)),
        ],
        cost_estimate=pl.CostEstimate(
            flops=6 * depth * size * (depth + size), bytes_accessed=6 * depth * (depth + size), transcendentals=0
        ),
        name="near",
        compiler_params=pltpu.CompilerParams(vmem_limit_bytes=20 << 20),
    )(in_hbm(x), in_hbm(y), keep, send, cross)


def far_product_kernel(x_ref, y_ref, keep_ref, *refs):
    got_ref, (out_ref, held_ref, sems) = (refs[0] if len(refs) == 4 else None), refs[-3:]
    chip, core = position()
    half = held_ref.shape[1]
    holder = 1 - core if got_ref is None else core
    waits = fetch((x_ref, y_ref), chip == 0, (1 - chip) * 2 + holder, held_ref, sems, 0)
    for t, wait in enumerate(waits):
        wait()
        rows = slice(t * half, t * half + half)
        u = lax.dot_general(held_ref[t], keep_ref[...], NT, preferred_element_type=F32)
        if got_ref is not None:
            u = u + got_ref[rows, :].astype(F32)
        out_ref[rows, :] = u.astype(BF16)


def far_product(x, y, keep, *got):
    size, depth = keep.shape
    return pl.pallas_call(
        far_product_kernel,
        out_shape=jax.ShapeDtypeStruct((depth, size), BF16),
        in_specs=[ANY, ANY, VMEM] + [VMEM] * len(got),
        out_specs=VMEM,
        scratch_shapes=[pltpu.VMEM((2, depth // 2, depth), BF16), pltpu.SemaphoreType.DMA((2,))],
        cost_estimate=pl.CostEstimate(
            flops=2 * depth * depth * size, bytes_accessed=2 * depth * (depth + 2 * size), transcendentals=0
        ),
        name="far_product",
        compiler_params=pltpu.CompilerParams(vmem_limit_bytes=20 << 20),
    )(in_hbm(x), in_hbm(y), keep, *got)


def far_kernel(hands, sel_ref, both_ref, mine_ref, give_ref, total_ref):
    _, core = position()
    total_ref[...] = jnp.dot(sel_ref[...], both_ref[...], preferred_element_type=F32)
    deal_out(total_ref, hands, core, mine_ref, give_ref)


def select_columns(v, index):
    hot = (index[:, None] == lax.broadcasted_iota(jnp.int32, (index.shape[0], v.shape[1]), 1)).astype(BF16)
    return lax.dot_general(hot, v, NT, preferred_element_type=F32).astype(BF16)


def place(own, dest, groups):
    source = jnp.argmax(dest[None, :] == jnp.arange(groups, dtype=dest.dtype)[:, None], axis=1)
    pieces = own.reshape(groups, own.shape[0] // groups, own.shape[1])
    pieces = lax.all_to_all(pieces, "blk", 0, 0)
    pieces = jnp.take(pieces, source, axis=0)
    pieces = lax.all_to_all(pieces, "blk", 0, 0)
    return pieces.reshape(own.shape)


def two_chips(x, y, v, index, orders, dest):
    slabs, groups = lax.axis_size("slab"), lax.axis_size("blk")
    depth, size = v.shape[0], index.shape[1]
    hands = deal(size)
    top = len(hands[0][0]) * LANES
    to_core = [(s, s ^ 1) for s in range(slabs)]
    to_chip = [(s, s ^ 2) for s in range(slabs)]
    blocks = jax.ShapeDtypeStruct(packed_shape(hands), F32)
    chip, core = position()
    first, second = index

    send = lax.optimization_barrier(select_columns(v, jnp.where(chip == 0, second, first)))
    far = lax.ppermute(send, "slab", to_chip)
    keep = select_columns(v, jnp.where(chip == 0, first, second))
    cross = lax.ppermute(jnp.where(core == 0, send, keep), "slab", to_core)
    give = far_product(x, y, keep)
    got = lax.ppermute(give, "slab", to_core)
    side_mine, side_give, main_mine, main_give = near(hands, x, y, keep, send, cross)
    side_sum = side_mine + lax.ppermute(side_give, "slab", to_core)
    early = lax.ppermute(side_sum, "slab", to_chip)
    both = far_product(x, y, keep, got)
    main_sum = main_mine + lax.ppermute(main_give, "slab", to_core)
    far_mine, far_give = pl.pallas_call(
        functools.partial(far_kernel, hands),
        out_shape=(blocks, blocks),
        in_specs=[VMEM] * 2,
        out_specs=(VMEM, VMEM),
        scratch_shapes=[pltpu.VMEM((size, size), F32)],
        cost_estimate=pl.CostEstimate(
            flops=2 * depth * size * size, bytes_accessed=4 * depth * size, transcendentals=0
        ),
        name="far",
        compiler_params=pltpu.CompilerParams(vmem_limit_bytes=8 << 20),
    )(far, both)
    total = main_sum + early + (far_mine + lax.ppermute(far_give, "slab", to_core))
    first_got = lax.ppermute(total[:top], "slab", to_chip)
    rest_got = lax.ppermute(total[top:], "slab", to_chip)
    schur = total[:top] * first_got
    other = lax.ppermute(schur, "slab", to_core)
    upper = pl.pallas_call(
        functools.partial(factor_first_kernel, hands),
        out_shape=jax.ShapeDtypeStruct((LANES, size), F32),
        in_specs=[SMEM, VMEM, VMEM],
        out_specs=VMEM,
        cost_estimate=pl.CostEstimate(
            flops=LANES * LANES * size, bytes_accessed=16 * LANES * size, transcendentals=LANES
        ),
        name="factor_first",
        compiler_params=pltpu.CompilerParams(vmem_limit_bytes=8 << 20),
    )(orders, schur, other)
    schur_rest = total[top:] * rest_got
    other_rest = lax.ppermute(schur_rest, "slab", to_core)
    own = pl.pallas_call(
        functools.partial(factor_rest_kernel, hands),
        out_shape=jax.ShapeDtypeStruct((size // slabs, size), F32),
        in_specs=[SMEM] + [VMEM] * 5,
        out_specs=VMEM,
        scratch_shapes=[pltpu.VMEM((size, size), F32)],
        name="factor_rest",
        compiler_params=pltpu.CompilerParams(vmem_limit_bytes=8 << 20),
    )(orders, upper, schur, other, schur_rest, other_rest)
    return place(own, dest, groups)


def any_chips(x, y, v, index, orders, dest):
    slabs, groups = lax.axis_size("slab"), lax.axis_size("blk")
    first, second = index
    order = orders[lax.axis_index("blk")]
    size = first.shape[0]
    share = size // slabs
    slab = lax.axis_index("slab")
    row_start = slab * share

    def pairing(z, index):
        picked = select_columns(v, index)
        every = lax.all_gather(picked, "slab", axis=1, tiled=True)
        c = jnp.dot(every, z, preferred_element_type=F32).astype(BF16)
        return lax.dot_general(c, picked, NT, preferred_element_type=F32)

    both = jnp.concatenate([pairing(x, first), pairing(y, second)], axis=1)
    both = lax.psum_scatter(both, "slab", scatter_dimension=0, tiled=True)
    schur = both[:, :size] * both[:, size:]
    row_ids = row_start + jnp.arange(share, dtype=jnp.int32)
    col_ids = jnp.arange(size, dtype=jnp.int32)
    mask = (row_ids[:, None] < order) & (col_ids[None, :] < order)
    schur = jnp.where(mask, schur, 0.0) + (row_ids[:, None] == col_ids[None, :]).astype(F32)
    whole = lax.all_gather(schur, "slab", axis=0, tiled=True)
    whole = 0.5 * (whole + whole.T)
    own = pl.pallas_call(
        factor_whole_kernel,
        out_shape=jax.ShapeDtypeStruct((share, size), F32),
        in_specs=[VMEM],
        out_specs=VMEM,
        scratch_shapes=[pltpu.VMEM((size, size), F32)],
        name="factor",
        compiler_params=pltpu.CompilerParams(vmem_limit_bytes=8 << 20),
    )(whole)
    return place(own, dest, groups)


def on_device(xinv, ymat, basis, pair_index, orders, dest):
    body = two_chips if lax.axis_size("slab") == 4 else any_chips
    return body(xinv[0], ymat[0], basis[0], pair_index[0], orders, dest)[None]


def solution(mesh):
    return jax.shard_map(
        on_device,
        mesh=mesh,
        in_specs=(
            P("blk", None, "slab"),
            P("blk", None, "slab"),
            P("blk", "slab", None),
            P("blk", None, None),
            P(),
            P(),
        ),
        out_specs=P("blk", "slab", None),
        check_vma=False,
    )
```
